128 devices in a mesh: tiles: 16 (over y, z), rows: 8 (over x, core).
Axes of the slice: x: 4, y: 4, z: 4, core: 2. Of those that a mesh axis runs over, the one named last changes fastest.
Arguments:
- tile_values: bfloat16 [512, 128, 128, 128], P(('tiles', 'rows')), may hold values from -6 to 6
- tile_coords: int32 [256, 3], replicated, may hold values from 0 to 127, as said below
- tile_owner: int32 [256], replicated, may hold values from 0 to 127, as said below
- factor_b: bfloat16 [16384, 128], P('rows')
- factor_c: bfloat16 [16384, 128], P('rows')
Outputs:
- factor_a: float32 [16384, 128], P('rows')
The draws below stay inside these ranges and needn't reach their ends.
Inputs may be any that keep to these rules, and one draw needn't show every extreme that they name: `tile_owner`: devices are numbered along tiles then rows. A device holds at most 4 tiles, and in every draw some device holds exactly 4; its tiles fill its first slots in increasing order of tile number. `tile_coords`: no two tiles have the same block indices.
All inputs are finite; a program needn't handle non-finite values.
Results may differ from the reference program's by a relative error of at most 0.0003.
Values may be sent and summed in bfloat16 or wider, within the bound.
No kernel may reach another device: no remote copies, remote signals or barrier semaphores. Data moves between devices by JAX's collectives and lax.ppermute only.
A program may use at most 128 MiB of HBM per device.

```python
import math
import jax
import jax.numpy as jnp
from jax import lax

MODE = 16384
R = 128
TB = 128
TILE_MEAN = 2
CAP = 4
NNZ = 256
NB = 128
DEVICES = 128


def draw_factor(key, salt):
    keys = jax.random.split(jax.random.fold_in(key, salt), 4)
    where_in = jnp.arange(MODE, dtype=jnp.float32) / MODE
    trend = 1.0 + 2.0 * where_in
    rough = 10.0 ** jax.random.uniform(keys[0], (MODE,), jnp.float32)
    column_scale = 10.0 ** (0.5 * jax.random.uniform(keys[1], (R,), jnp.float32))
    factor_scale = math.sqrt(TB / 128.0) / MODE
    entries = jax.random.normal(keys[2], (MODE, R), jnp.float32)
    common = 0.9 * jax.random.normal(keys[3], (MODE, 1), jnp.float32)
    values = factor_scale * trend[:, None] * rough[:, None] * column_scale[None, :] * (entries + common)
    return values.astype(jnp.bfloat16)


def draw_factor_b(key, part):
    return draw_factor(key, 11)


def draw_factor_c(key, part):
    return draw_factor(key, 23)


def draw_tile_coords(key, part):
    chosen = jax.random.permutation(key, NB * NB * NB)[:NNZ].astype(jnp.int32)
    first = chosen // (NB * NB)
    second = chosen // NB % NB
    third = chosen % NB
    return jnp.stack([first, second, third], axis=1).astype(jnp.int32)


def draw_tile_owner(key, part):
    keys = jax.random.split(key, 3)
    device_count = NNZ // TILE_MEAN
    pair_count = device_count // 2
    moved = jax.random.randint(keys[0], (pair_count,), 0, TILE_MEAN + 1).astype(jnp.int32)
    moved = moved.at[0].set(TILE_MEAN)
    shuffled = jax.random.permutation(keys[1], device_count).astype(jnp.int32)
    counts = jnp.zeros((device_count,), jnp.int32)
    counts = counts.at[shuffled[0::2]].set(TILE_MEAN + moved)
    counts = counts.at[shuffled[1::2]].set(TILE_MEAN - moved)
    base = jnp.repeat(jnp.arange(device_count, dtype=jnp.int32), counts, total_repeat_length=NNZ)
    order = jax.random.permutation(keys[2], NNZ)
    return base[order].astype(jnp.int32)


def level_of(own_key, shape, cuts, low, high):
    def one(axis_at, parts):
        steps = jax.random.uniform(jax.random.fold_in(jax.random.fold_in(own_key, 6), axis_at), (parts,), jnp.float32, low / len(cuts), high / len(cuts))
        return jnp.repeat(jnp.exp(steps), shape[axis_at] // parts).reshape((-1,) + (1,) * (len(shape) - axis_at - 1))

    factor_of = one(*cuts[0])
    for cut in cuts[1:]:
        factor_of = factor_of * one(*cut)
    return factor_of


def noise(key, shape, width, limit, pieces=(), kind=jnp.bfloat16):
    result = width * jax.random.normal(key, shape, jnp.float32)
    if pieces:
        result = result * level_of(key, shape, pieces, -0.22, 0.18)
    return jnp.clip(result, -limit, limit).astype(kind)


def setup_inputs(seed: int = 0) -> dict:
    key_of = jax.random.split(jax.random.key(seed), 6)
    return {
        "tile_values": noise(key_of[0], (DEVICES * CAP, TB, TB, TB), 1.0, 6.0, ((0, 128),)),
        "tile_coords": draw_tile_coords(jax.random.fold_in(key_of[5], 71), 0),
        "tile_owner": draw_tile_owner(jax.random.fold_in(key_of[5], 71), 0),
        "factor_b": draw_factor_b(jax.random.fold_in(key_of[5], 71), 0),
        "factor_c": draw_factor_c(jax.random.fold_in(key_of[5], 71), 0),
    }


def reference(tile_values, tile_coords, tile_owner, factor_b, factor_c):
    same_owner = tile_owner[:, None] == tile_owner[None, :]
    earlier = jnp.arange(NNZ, dtype=jnp.int32)[None, :] < jnp.arange(NNZ, dtype=jnp.int32)[:, None]
    position = jnp.sum((same_owner & earlier).astype(jnp.int32), axis=1)
    slot = (tile_owner * CAP + position).astype(jnp.int32)

    def accumulate(total, inputs):
        which, coords = inputs
        tile = lax.dynamic_index_in_dim(tile_values, which, 0, keepdims=False).reshape(TB * TB, TB)
        block_c = lax.dynamic_slice_in_dim(factor_c, (coords[2] * TB).astype(jnp.int32), TB, 0)
        block_b = lax.dynamic_slice_in_dim(factor_b, (coords[1] * TB).astype(jnp.int32), TB, 0)
        inner = jnp.dot(tile.astype(jnp.float32), block_c.astype(jnp.float32), preferred_element_type=jnp.float32).reshape(TB, TB, R)
        contrib = jnp.sum(inner * block_b.astype(jnp.float32)[None, :, :], axis=1)
        first_row = (coords[0] * TB).astype(jnp.int32)
        current = lax.dynamic_slice_in_dim(total, first_row, TB, 0)
        return (lax.dynamic_update_slice_in_dim(total, current + contrib, first_row, 0), None)
    mttkrp, _ = lax.scan(accumulate, jnp.zeros((MODE, R), jnp.float32), (slot, tile_coords))
    dims = (((0,), (0,)), ((), ()))
    gram_b = lax.dot_general(factor_b.astype(jnp.float32), factor_b.astype(jnp.float32), dims, preferred_element_type=jnp.float32)
    gram_c = lax.dot_general(factor_c.astype(jnp.float32), factor_c.astype(jnp.float32), dims, preferred_element_type=jnp.float32)
    normal = gram_b * gram_c
    lower = jnp.linalg.cholesky(normal)
    return jax.scipy.linalg.cho_solve((lower, True), mttkrp.T).T
```

```python
import jax
import jax.numpy as jnp
from jax import lax
from jax.experimental import pallas as pl
from jax.experimental.pallas import tpu as pltpu
from jax.sharding import PartitionSpec as P

F32 = jnp.float32
BF16 = jnp.bfloat16
HIGHEST = lax.Precision.HIGHEST
STRIP = 8
PRESENT = 21
CHUNK = 16
BUFFERS = 8


def split3(x):
    hi = x.astype(BF16)
    rest = x - hi.astype(F32)
    mid = rest.astype(BF16)
    lo = (rest - mid.astype(F32)).astype(BF16)
    return hi, mid, lo


def join3(hi, mid, lo):
    return (lo.astype(F32) + mid.astype(F32)) + hi.astype(F32)


def vmem():
    return pl.BlockSpec(memory_space=pltpu.VMEM)


def smem():
    return pl.BlockSpec(memory_space=pltpu.SMEM)


def hbm():
    return pl.BlockSpec(memory_space=pl.ANY)


def slot_codes(tile_coords, tile_owner, slot_count, rows_count, tiles_count, rows_index):
    tiles = tile_owner.shape[0]
    number = jnp.arange(tiles, dtype=jnp.int32)
    earlier = (tile_owner[None, :] == tile_owner[:, None]) & (number[None, :] < number[:, None])
    order = jnp.sum(earlier.astype(jnp.int32), axis=1)
    slot = tile_owner * slot_count + order
    code = (
        tile_coords[:, 0]
        + (tile_coords[:, 1] << 7)
        + (tile_coords[:, 2] << 14)
        + (1 << PRESENT)
    )
    place = jnp.arange(tiles_count * slot_count, dtype=jnp.int32)
    wanted = ((place // slot_count) * rows_count + rows_index) * slot_count + place % slot_count
    return jnp.sum(jnp.where(slot[None, :] == wanted[:, None], code[None, :], 0), axis=1)


def pack_factors(fb_ref, fc_ref, sb_ref, sc_ref, out_ref, strips, gram, sem):
    t = lax.axis_index("tiles")
    blocks = sb_ref.shape[0]
    copies = [
        pltpu.make_async_copy(sb_ref.at[:, t], strips.at[pl.ds(0, blocks)], sem.at[0]),
        pltpu.make_async_copy(sc_ref.at[:, t], strips.at[pl.ds(blocks, blocks)], sem.at[1]),
    ]
    for copy in copies:
        copy.start()
    parts = []
    for at, ref in enumerate((fb_ref, fc_ref)):
        rows = ref[...]
        gram[at] = lax.dot_general(rows, rows, (((0,), (0,)), ((), ())), preferred_element_type=F32)
        parts.extend(split3(gram[at, pl.ds(pl.multiple_of(t * STRIP, STRIP), STRIP), :]))
    for copy in copies:
        copy.wait()
    held = strips[...]
    for d in range(out_ref.shape[0]):
        out_ref[d, 0 : 2 * blocks] = held
        for at, part in enumerate(parts):
            out_ref[d, 2 * blocks + at] = part


def route_factors(code_ref, in_ref, out_ref, *, slots):
    sources = in_ref.shape[0]
    blocks = (in_ref.shape[1] - 6) // 2
    for d in range(out_ref.shape[0]):
        for s in range(slots):
            code = code_ref[d * slots + s]
            j = (code >> 7) & 127
            k = (code >> 14) & 127
            out_ref[d, s] = in_ref[j // blocks, j % blocks]
            out_ref[d, slots + s] = in_ref[k // blocks, blocks + k % blocks]
    grams = []
    for at in range(2):
        base = 2 * blocks + 3 * at
        total = None
        for q in range(sources):
            piece = join3(in_ref[q, base], in_ref[q, base + 1], in_ref[q, base + 2])
            total = piece if total is None else total + piece
        grams.append(total)
    for at, part in enumerate(split3(grams[0] * grams[1])):
        for d in range(out_ref.shape[0]):
            out_ref[d, 2 * slots + at] = part


def contract(code_ref, x_ref, in_ref, out_ref, normal_ref, buf, bs, cs, sem, *, slots):
    t = lax.axis_index("tiles")
    edge = x_ref.shape[1]
    per_tile = edge // CHUNK
    strips = edge // STRIP
    live = code_ref[t * slots] >> PRESENT
    for s in range(1, slots):
        live = live + (code_ref[t * slots + s] >> PRESENT)
    chunks = live * per_tile

    def fetch(c):
        s = c // per_tile
        a = (c % per_tile) * CHUNK
        slot = c % BUFFERS
        return pltpu.make_async_copy(
            x_ref.at[s, pl.ds(a, CHUNK)], buf.at[slot], sem.at[slot]
        )

    for c in range(BUFFERS):
        @pl.when(c < chunks)
        def _():
            fetch(jnp.int32(c)).start()

    for s in range(slots):
        for u in range(strips):
            bs[s, pl.ds(u * STRIP, STRIP), :] = in_ref[u, s].astype(F32)
            cs[s, pl.ds(u * STRIP, STRIP), :] = in_ref[u, slots + s].astype(F32)
    for u in range(strips):
        normal_ref[pl.ds(u * STRIP, STRIP), :] = join3(
            in_ref[u, 2 * slots], in_ref[u, 2 * slots + 1], in_ref[u, 2 * slots + 2]
        )
    out_ref[...] = jnp.zeros_like(out_ref)

    def step(c, carry):
        s = c // per_tile
        slot = c % BUFFERS
        fetch(c).wait()
        x = buf[slot].reshape(CHUNK * edge, edge)
        inner = jnp.dot(x, cs[s].astype(BF16), preferred_element_type=F32)
        inner = inner.reshape(CHUNK, edge, edge) * bs[s][None]
        total = jnp.sum(inner, axis=1)
        for u in range(CHUNK // STRIP):
            out_ref[(c % per_tile) * (CHUNK // STRIP) + u, s] = total[u * STRIP : (u + 1) * STRIP]

        @pl.when(c + BUFFERS < chunks)
        def _():
            fetch(c + BUFFERS).start()

        return carry

    lax.fori_loop(0, chunks, step, 0)


def gather_blocks(code_ref, in_ref, out_ref, *, slots):
    out_ref[...] = jnp.zeros_like(out_ref)
    blocks = out_ref.shape[1]
    for d in range(in_ref.shape[0]):
        for s in range(slots):
            code = code_ref[d * slots + s]
            i = code & 127
            here = (code >> PRESENT) > 0
            value = jnp.where(here, in_ref[d, s], 0.0)
            out_ref[i // blocks, i % blocks] += value


def solve(in_ref, inv_ref, out_ref):
    total = in_ref[0]
    for q in range(1, in_ref.shape[0]):
        total = total + in_ref[q]
    rows = total.reshape(total.shape[0] * STRIP, total.shape[2])
    inv = inv_ref[...]
    first = lax.dot_general(
        rows, inv, (((1,), (1,)), ((), ())), precision=HIGHEST, preferred_element_type=F32
    )
    second = jnp.dot(first, inv, precision=HIGHEST, preferred_element_type=F32)
    second = second.reshape(total.shape)
    for d in range(out_ref.shape[0]):
        out_ref[d] = second


def body(tile_values, tile_coords, tile_owner, factor_b, factor_c):
    slots = tile_values.shape[0]
    edge = tile_values.shape[1]
    rank = factor_b.shape[1]
    shard = factor_b.shape[0]
    tiles_count = lax.axis_size("tiles")
    rows_count = lax.axis_size("rows")
    rows_index = lax.axis_index("rows")
    blocks = shard // edge
    strips = edge // STRIP
    tile = (STRIP, rank)

    packed = pl.pallas_call(
        pack_factors,
        name="pack_factors",
        out_shape=jax.ShapeDtypeStruct((rows_count, 2 * blocks + 6) + tile, BF16),
        in_specs=[vmem(), vmem(), hbm(), hbm()],
        out_specs=vmem(),
        scratch_shapes=[
            pltpu.VMEM((2 * blocks,) + tile, BF16),
            pltpu.VMEM((2, rank, rank), F32),
            pltpu.SemaphoreType.DMA((2,)),
        ],
    )(
        factor_b,
        factor_c,
        factor_b.reshape((blocks, strips) + tile),
        factor_c.reshape((blocks, strips) + tile),
    )
    codes = slot_codes(tile_coords, tile_owner, slots, rows_count, tiles_count, rows_index)
    spread = lax.all_to_all(packed, "rows", 0, 0, tiled=True)
    routed = pl.pallas_call(
        lambda *refs: route_factors(*refs, slots=slots),
        name="route_factors",
        out_shape=jax.ShapeDtypeStruct((tiles_count, 2 * slots + 3) + tile, BF16),
        in_specs=[smem(), vmem()],
        out_specs=vmem(),
    )(codes, spread)
    chosen = lax.all_to_all(routed, "tiles", 0, 0, tiled=True)
    partials, normal = pl.pallas_call(
        lambda *refs: contract(*refs, slots=slots),
        name="contract",
        out_shape=(
            jax.ShapeDtypeStruct((tiles_count, slots) + tile, F32),
            jax.ShapeDtypeStruct((rank, rank), F32),
        ),
        in_specs=[smem(), hbm(), vmem()],
        out_specs=(vmem(), vmem()),
        scratch_shapes=[
            pltpu.VMEM((BUFFERS, CHUNK, edge, edge), BF16),
            pltpu.VMEM((slots, edge, rank), F32),
            pltpu.VMEM((slots, edge, rank), F32),
            pltpu.SemaphoreType.DMA((BUFFERS,)),
        ],
        compiler_params=pltpu.CompilerParams(vmem_limit_bytes=32 << 20),
    )(codes, tile_values, chosen)
    moved = lax.all_to_all(partials, "tiles", 0, 0, tiled=True)
    lower = jnp.linalg.cholesky(normal)
    inverse = lax.linalg.triangular_solve(
        lower, jnp.eye(rank, dtype=F32), left_side=True, lower=True
    )
    dense = pl.pallas_call(
        lambda *refs: gather_blocks(*refs, slots=slots),
        name="gather_blocks",
        out_shape=jax.ShapeDtypeStruct((rows_count, blocks) + tile, F32),
        in_specs=[smem(), vmem()],
        out_specs=vmem(),
    )(codes, moved)
    owned = lax.all_to_all(dense, "rows", 0, 0, tiled=True)
    solved = pl.pallas_call(
        solve,
        name="solve",
        out_shape=jax.ShapeDtypeStruct((tiles_count, blocks) + tile, F32),
        in_specs=[vmem(), vmem()],
        out_specs=vmem(),
    )(owned, inverse)
    full = lax.all_to_all(solved, "tiles", 0, 0, tiled=True)
    return full.transpose(1, 0, 2, 3).reshape(shard, rank)


def solution(mesh):
    in_specs = (P(("tiles", "rows"), None, None, None), P(), P(), P("rows", None), P("rows", None))
    out_specs = P("rows", None)
    return jax.shard_map(body, mesh=mesh, in_specs=in_specs, out_specs=out_specs, check_vma=False)
```

```python
import jax
import jax.numpy as jnp
from jax import lax
from jax.experimental import pallas as pl
from jax.experimental.pallas import tpu as pltpu
from jax.sharding import PartitionSpec as P

F32 = jnp.float32
BF16 = jnp.bfloat16
HIGHEST = lax.Precision.HIGHEST
STRIP = 8
PRESENT = 21
CHUNK = 16
PARTS = 4
LANES = 128
BITS = 15.0
FULL = 32768.0
TINY = 2.0**-111
CAPACITIES = (6, 2)
CORES = 2
SMALL = pl.CostEstimate(flops=1024, bytes_accessed=1024, transcendentals=0)
LIMIT = pltpu.CompilerParams(vmem_limit_bytes=8 << 20)


def vmem():
    return pl.BlockSpec(memory_space=pltpu.VMEM)


def smem():
    return pl.BlockSpec(memory_space=pltpu.SMEM)


def hbm():
    return pl.BlockSpec(memory_space=pl.ANY)


def in_hbm(x):
    return pltpu.with_memory_space_constraint(x, pltpu.HBM)


def coord_i(code):
    return code & 127


def coord_j(code):
    return (code >> 7) & 127


def coord_k(code):
    return (code >> 14) & 127


def present(code):
    return code >> PRESENT


def plan(owner_hbm, coords_hbm, code_ref, rounds_ref, owner_ref, coords_ref, sem, *, slots, rows_count, blocks):
    t = lax.axis_index("tiles")
    r = lax.axis_index("rows")
    tiles = owner_ref.shape[1]
    chips = rows_count // CORES
    shift = (blocks * CORES).bit_length() - 1
    loads = [
        pltpu.make_async_copy(owner_hbm, owner_ref, sem.at[0]),
        pltpu.make_async_copy(coords_hbm, coords_ref, sem.at[1]),
    ]
    for load in loads:
        load.start()
    for load in loads:
        load.wait()
    owner = owner_ref[...]
    coords = coords_ref[...]
    first, second, third = coords[0:1], coords[1:2], coords[2:3]
    code = first + (second << 7) + (third << 14) + (1 << PRESENT)
    key_b = owner * chips + (second >> shift)
    key_c = owner * chips + (third >> shift)
    lanes = jnp.concatenate([owner, code, key_b, key_c, owner, code, key_b, key_c], axis=0)
    columns = jnp.transpose(lanes)
    owner_at, code_at = columns[:, 0:1], columns[:, 1:2]
    key_b_at, key_c_at = columns[:, 2:3], columns[:, 3:4]
    square = (tiles, tiles)
    number_at = lax.broadcasted_iota(jnp.int32, square, 0)
    number = lax.broadcasted_iota(jnp.int32, square, 1)
    one = jnp.ones(square, jnp.int32)
    zero = jnp.zeros(square, jnp.int32)
    earlier = jnp.where((owner_at == owner) & (number < number_at), one, zero)
    slot_at = owner_at * slots + jnp.sum(earlier, axis=1, keepdims=True)
    place = lax.broadcasted_iota(jnp.int32, (1, LANES), 1)
    within = place % slots
    column = ((place // slots) * rows_count + r) * slots + within
    row = (t * rows_count + (place - 64) // slots) * slots + within
    wanted = jnp.where(place < 64, column, jnp.where(place < 96, row, -1))
    code_ref[...] = jnp.sum(jnp.where(slot_at == wanted, code_at, 0), axis=0, keepdims=True)
    most = jnp.zeros((1, 1), jnp.int32)
    for key_at in (key_b_at, key_c_at):
        same = jnp.where(key_at == key_b, one, zero) + jnp.where(key_at == key_c, one, zero)
        most = jnp.maximum(most, jnp.max(jnp.sum(same, axis=1, keepdims=True), axis=0, keepdims=True))
    rounds = jnp.zeros((1, 1), jnp.int32)
    base = 0
    for capacity in CAPACITIES[:-1]:
        base = base + capacity
        rounds = rounds + jnp.where(most > base, 1, 0)
    rounds_ref[0, 0] = jnp.sum(rounds)


def gather_factors(code_ref, fb_ref, fc_ref, sb_ref, sc_ref, *refs, slots):
    outs, sem = refs[:-1], refs[-1]
    r = lax.axis_index("rows")
    blocks = fb_ref.shape[0]
    count = jnp.int32(0)
    for x in range(outs[0].shape[0]):
        at = jnp.int32(0)
        for s in range(slots):
            code = code_ref[0, 64 + (x * CORES + r % CORES) * slots + s]
            for own, sibling, coord in ((fb_ref, sb_ref, coord_j(code)), (fc_ref, sc_ref, coord_k(code))):
                shard = coord // blocks
                hit = (present(code) > 0) & (shard // CORES == r // CORES)
                base = 0
                for out, capacity in zip(outs, CAPACITIES):
                    if base >= 2 * s + 2:
                        break
                    inside = hit & (at >= base) & (at < base + capacity)
                    for ref, held in ((own, shard == r), (sibling, shard != r)):

                        @pl.when(inside & held)
                        def _(ref=ref, coord=coord, at=at, x=x, out=out, base=base):
                            pltpu.make_async_copy(
                                ref.at[coord % blocks], out.at[x, at - base], sem
                            ).start()

                    base = base + capacity
                at = at + hit.astype(jnp.int32)
        count = count + at

    def drain(_, carry):
        pltpu.make_async_copy(fb_ref.at[0], outs[0].at[0, 0], sem).wait()
        return carry

    lax.fori_loop(0, count, drain, 0)


def chip_gram(fb_ref, fc_ref, sb_ref, sc_ref, out_ref, buf, sem):
    core = lax.axis_index("rows") % CORES
    over = (((0,), (0,)), ((), ()))
    for which, (own, sibling) in enumerate(((fb_ref, sb_ref), (fc_ref, sc_ref))):

        @pl.when(core == which)
        def _(own=own, sibling=sibling):
            copies = [
                pltpu.make_async_copy(ref, buf.at[at], sem.at[at])
                for at, ref in enumerate((own, sibling))
            ]
            for copy in copies:
                copy.start()
            for copy in copies:
                copy.wait()

    out_ref[...] = sum(
        lax.dot_general(buf[at], buf[at], over, preferred_element_type=F32) for at in range(CORES)
    )


def contract(code_ref, x_ref, *refs, slots, blocks):
    ins = refs[: len(CAPACITIES)]
    out_ref, buf, bs, cs, scalar_ref, code_sem, sem = refs[len(CAPACITIES) :]
    r = lax.axis_index("rows")
    edge = x_ref.shape[1]
    part = edge // PARTS

    def fetch(s, q):
        rows = pl.ds(q * part, part)
        return pltpu.make_async_copy(x_ref.at[s, rows], buf.at[s, rows], sem.at[s, q])

    codes_copy = pltpu.make_async_copy(code_ref, scalar_ref, code_sem)
    codes_copy.start()
    for s in range(slots):
        for q in range(PARTS):
            fetch(s, q).start()
    codes_copy.wait()
    codes = [scalar_ref[0, 64 + r * slots + s] for s in range(slots)]
    live = jnp.int32(0)
    for code in codes:
        live = live + present(code)
    chips = []
    for s, code in enumerate(codes):
        for coord, keep in ((coord_j(code), bs), (coord_k(code), cs)):
            chip = coord // (blocks * CORES)
            at = jnp.int32(0)
            for other in chips:
                at = at + (other == chip).astype(jnp.int32)
            chips.append(chip)
            at = jnp.where(present(code) > 0, at, 0)
            base = 0
            value = None
            for ref, capacity in zip(ins, CAPACITIES):
                if base >= 2 * s + 2:
                    break
                inside = (at >= base) & (at < base + capacity)
                held = ref[chip, jnp.where(inside, at - base, 0)].astype(F32)
                value = held if value is None else jnp.where(inside, held, value)
                base = base + capacity
            keep[s] = value.astype(keep.dtype)
    out_ref[...] = jnp.zeros_like(out_ref)

    def multiply(s, q):
        b = bs[s]
        c = cs[s]
        for a in range(q * part, (q + 1) * part, CHUNK):
            x = buf[s, a : a + CHUNK].reshape(CHUNK * edge, edge)
            inner = jnp.dot(x, c, preferred_element_type=F32).reshape(CHUNK, edge, edge)
            total = jnp.sum(inner * b[None], axis=1)
            for u in range(CHUNK // STRIP):
                out_ref[a // STRIP + u, s] = total[u * STRIP : (u + 1) * STRIP]

    def whole(s, carry):
        for q in range(PARTS):
            fetch(s, q).wait()
        for q in range(PARTS):
            multiply(s, q)
        return carry

    last = live - 1
    lax.fori_loop(0, last, whole, 0)

    @pl.when(live > 0)
    def _():
        for q in range(PARTS):
            fetch(last, q).wait()
            multiply(last, q)

    def drain(s, carry):
        for q in range(PARTS):
            fetch(s, q).wait()
        return carry

    lax.fori_loop(live, slots, drain, 0)


def eliminate(matrix):
    size = matrix.shape[0]
    down = lax.broadcasted_iota(jnp.int32, (size, size), 0)
    across = lax.broadcasted_iota(jnp.int32, (size, size), 1)
    eye = jnp.where(down == across, 1.0, 0.0).astype(F32)
    both = jnp.concatenate([matrix, eye], axis=1)
    below = lax.broadcasted_iota(jnp.int32, (size, 1), 0)
    for k in range(size):
        top = k // STRIP * STRIP
        rest = both[top:]
        row = both[k : k + 1]
        factor = rest[:, k : k + 1] * (1.0 / both[k : k + 1, k : k + 1])
        factor = jnp.where(below[top:] > k, factor, 0.0)
        rest = rest - factor * row
        both = rest if top == 0 else jnp.concatenate([both[:top], rest], axis=0)
    pivots = jnp.sum(jnp.where(down == across, both[:, :size], 0.0), axis=1, keepdims=True)
    return both[:, size:] * lax.rsqrt(pivots)


def times(a, b, over=((1,), (0,))):
    return lax.dot_general(a, b, (over, ((), ())), precision=HIGHEST, preferred_element_type=F32)


def factor_first(one_ref, other_ref, first_ref, side_ref, rest_ref):
    normal = one_ref[...] * other_ref[...]
    half = normal.shape[0] // 2
    first = eliminate(normal[:half, :half])
    side = times(normal[half:, :half], first, ((1,), (1,)))
    first_ref[...] = first
    side_ref[...] = side
    rest_ref[...] = normal[half:, half:] - times(side, side, ((1,), (1,)))


def factor_second(first_ref, side_ref, rest_ref, out_ref):
    first = first_ref[...]
    half = first.shape[0]
    second = eliminate(rest_ref[...])
    out_ref[:half, :half] = first
    out_ref[:half, half:] = jnp.zeros((half, half), F32)
    out_ref[half:, :half] = -times(times(second, side_ref[...]), first)
    out_ref[half:, half:] = second


def gather_blocks(code_ref, in_ref, out_ref, *, slots):
    out_ref[...] = jnp.zeros_like(out_ref)
    blocks = out_ref.shape[1]
    for d in range(in_ref.shape[0]):
        for s in range(slots):
            code = code_ref[0, d * slots + s]
            i = coord_i(code)
            value = jnp.where(present(code) > 0, in_ref[d, s], 0.0)
            out_ref[i // blocks, i % blocks] += value


def solve(in_ref, inv_ref, out_ref):
    total = in_ref[0]
    for q in range(1, in_ref.shape[0]):
        total = total + in_ref[q]
    blocks = total.shape[0]
    rows = total.reshape(blocks * STRIP, total.shape[2])
    inv = inv_ref[...]
    solved = times(times(rows, inv, ((1,), (1,))), inv).reshape(total.shape)
    largest = jnp.max(jnp.abs(solved), axis=2, keepdims=True)
    exponent = jnp.ceil(jnp.log2(jnp.maximum(largest, TINY)))
    scaled = solved * jnp.exp2(BITS - exponent)
    fixed = jnp.clip(jnp.round(scaled), 1 - FULL, FULL - 1).astype(jnp.int32).astype(jnp.int16)
    lane = lax.broadcasted_iota(jnp.int32, solved.shape[1:], 1)
    exponents = jnp.zeros(solved.shape[1:], F32)
    for b in range(blocks):
        exponents = jnp.where(lane == b, exponent[b], exponents)
    exponents = exponents.astype(jnp.int32).astype(jnp.int16)
    for d in range(out_ref.shape[0]):
        out_ref[d, :blocks] = fixed
        out_ref[d, blocks] = exponents


def unpack(in_ref, out_ref):
    blocks = out_ref.shape[0]
    for t in range(in_ref.shape[0]):
        scale = jnp.exp2(in_ref[t, blocks].astype(jnp.int32).astype(F32) - BITS)
        for b in range(blocks):
            out_ref[b, t] = in_ref[t, b].astype(jnp.int32).astype(F32) * scale[:, b : b + 1]


def body(tile_values, tile_coords, tile_owner, factor_b, factor_c):
    slots = tile_values.shape[0]
    edge = tile_values.shape[1]
    rank = factor_b.shape[1]
    shard = factor_b.shape[0]
    tiles_count = lax.axis_size("tiles")
    rows_count = lax.axis_size("rows")
    blocks = shard // edge
    tile = (STRIP, rank)
    half = (rank // 2, rank // 2)

    chips = rows_count // CORES

    def from_peer(x, peer):
        return lax.ppermute(x, "rows", [(q, peer(q)) for q in range(rows_count)])

    def swap(x):
        groups = [[x * CORES + core for x in range(chips)] for core in range(CORES)]
        return lax.all_to_all(x, "rows", 0, 0, axis_index_groups=groups, tiled=True)

    sibling_b, sibling_c = (from_peer(f, lambda q: q ^ 1) for f in (factor_b, factor_c))
    codes, rounds = pl.pallas_call(
        lambda *refs: plan(*refs, slots=slots, rows_count=rows_count, blocks=blocks),
        name="plan",
        out_shape=(
            jax.ShapeDtypeStruct((1, LANES), jnp.int32),
            jax.ShapeDtypeStruct((1, 1), jnp.int32),
        ),
        in_specs=[pl.BlockSpec(memory_space=pltpu.HBM)] * 2,
        out_specs=(vmem(), smem()),
        scratch_shapes=[
            pltpu.VMEM((1, tile_owner.shape[0]), jnp.int32),
            pltpu.VMEM((3, tile_owner.shape[0]), jnp.int32),
            pltpu.SemaphoreType.DMA((2,)),
        ],
        compiler_params=LIMIT,
    )(in_hbm(tile_owner.reshape(1, -1)), in_hbm(tile_coords.T))
    by_block = lambda f: f.reshape(blocks, edge, rank)
    sent = pl.pallas_call(
        lambda *refs: gather_factors(*refs, slots=slots),
        name="gather_factors",
        out_shape=tuple(jax.ShapeDtypeStruct((chips, c, edge, rank), BF16) for c in CAPACITIES),
        in_specs=[smem()] + [hbm()] * 4,
        out_specs=(vmem(),) * len(CAPACITIES),
        scratch_shapes=[pltpu.SemaphoreType.DMA],
        compiler_params=LIMIT,
    )(
        codes,
        in_hbm(by_block(factor_b)),
        in_hbm(by_block(factor_c)),
        by_block(sibling_b),
        by_block(sibling_c),
    )
    rest = lax.cond(rounds[0, 0] > 0, swap, lambda x: x, sent[1])
    first, rest = lax.optimization_barrier((sent[0], rest))
    chosen = [swap(first), rest]
    own_b, own_c, sibling_b, sibling_c, *sent = lax.optimization_barrier(
        (factor_b, factor_c, sibling_b, sibling_c, *sent)
    )
    gram = pl.pallas_call(
        chip_gram,
        name="chip_gram",
        out_shape=jax.ShapeDtypeStruct((rank, rank), F32),
        in_specs=[hbm()] * 4,
        out_specs=vmem(),
        scratch_shapes=[
            pltpu.VMEM((CORES, shard, rank), BF16),
            pltpu.SemaphoreType.DMA((CORES,)),
        ],
        compiler_params=LIMIT,
        cost_estimate=SMALL,
    )(in_hbm(own_b), in_hbm(own_c), sibling_b, sibling_c)
    away = [from_peer(gram, lambda q: (q + step) % rows_count) for step in range(CORES, rows_count, CORES)]
    gram = gram + sum(away[1:], away[0])
    chosen, gram = lax.optimization_barrier((chosen, gram))
    other = from_peer(gram, lambda q: q ^ 1)

    partials = pl.pallas_call(
        lambda *refs: contract(*refs, slots=slots, blocks=blocks),
        name="contract",
        out_shape=jax.ShapeDtypeStruct((tiles_count, slots) + tile, F32),
        in_specs=[vmem(), pl.BlockSpec(memory_space=pltpu.HBM)] + [vmem()] * len(CAPACITIES),
        out_specs=vmem(),
        scratch_shapes=[
            pltpu.VMEM(tile_values.shape, BF16),
            pltpu.VMEM((slots, edge, rank), F32),
            pltpu.VMEM((slots, edge, rank), BF16),
            pltpu.SMEM((1, LANES), jnp.int32),
            pltpu.SemaphoreType.DMA,
            pltpu.SemaphoreType.DMA((slots, PARTS)),
        ],
        compiler_params=pltpu.CompilerParams(vmem_limit_bytes=24 << 20),
        cost_estimate=pl.CostEstimate(flops=slots * 2 * edge**4, bytes_accessed=slots * 2 * edge**3, transcendentals=0),
    )(codes, in_hbm(tile_values), *chosen)
    moved = lax.all_to_all(partials, "tiles", 0, 0, tiled=True)
    halves = pl.pallas_call(
        factor_first,
        name="factor_first",
        out_shape=(jax.ShapeDtypeStruct(half, F32),) * 3,
        in_specs=[vmem()] * 2,
        out_specs=(vmem(),) * 3,
        compiler_params=LIMIT,
        cost_estimate=pl.CostEstimate(flops=1 << 30, bytes_accessed=1 << 20, transcendentals=64),
    )(gram, other)
    moved, halves = lax.optimization_barrier((moved, halves))
    dense = pl.pallas_call(
        lambda *refs: gather_blocks(*refs, slots=slots),
        name="gather_blocks",
        out_shape=jax.ShapeDtypeStruct((rows_count, blocks) + tile, F32),
        in_specs=[smem(), vmem()],
        out_specs=vmem(),
        compiler_params=LIMIT,
    )(codes, moved)
    owned = lax.all_to_all(dense, "rows", 0, 0, tiled=True)
    inverse = pl.pallas_call(
        factor_second,
        name="factor_second",
        out_shape=jax.ShapeDtypeStruct((rank, rank), F32),
        in_specs=[vmem()] * 3,
        out_specs=vmem(),
        compiler_params=LIMIT,
        cost_estimate=pl.CostEstimate(flops=1 << 30, bytes_accessed=1 << 20, transcendentals=64),
    )(*halves)
    solved = pl.pallas_call(
        solve,
        name="solve",
        out_shape=jax.ShapeDtypeStruct((tiles_count, blocks + 1) + tile, jnp.int16),
        in_specs=[vmem(), vmem()],
        out_specs=vmem(),
        compiler_params=LIMIT,
    )(owned, inverse)
    full = lax.all_to_all(solved, "tiles", 0, 0, tiled=True)
    out = pl.pallas_call(
        unpack,
        name="unpack",
        out_shape=jax.ShapeDtypeStruct((blocks, tiles_count) + tile, F32),
        in_specs=[vmem()],
        out_specs=vmem(),
        compiler_params=LIMIT,
    )(full)
    return out.reshape(shard, rank)


def solution(mesh):
    in_specs = (P(("tiles", "rows"), None, None, None), P(), P(), P("rows", None), P("rows", None))
    out_specs = P("rows", None)
    return jax.shard_map(body, mesh=mesh, in_specs=in_specs, out_specs=out_specs, check_vma=False)
```

```python
import jax
import jax.numpy as jnp
from jax import lax
from jax.experimental import pallas as pl
from jax.experimental.pallas import tpu as pltpu
from jax.sharding import PartitionSpec as P

F32 = jnp.float32
BF16 = jnp.bfloat16
HIGHEST = lax.Precision.HIGHEST
STRIP = 8
PRESENT = 21
CHUNK = 16
PARTS = 4
LANES = 128
BITS = 15.0
FULL = 32768.0
TINY = 2.0**-111
CAPACITIES = (6, 2)
CORES = 2
SMALL = pl.CostEstimate(flops=1024, bytes_accessed=1024, transcendentals=0)
LIMIT = pltpu.CompilerParams(vmem_limit_bytes=8 << 20)


def vmem():
    return pl.BlockSpec(memory_space=pltpu.VMEM)


def smem():
    return pl.BlockSpec(memory_space=pltpu.SMEM)


def hbm():
    return pl.BlockSpec(memory_space=pl.ANY)


def in_hbm(x):
    return pltpu.with_memory_space_constraint(x, pltpu.HBM)


def coord_i(code):
    return code & 127


def coord_j(code):
    return (code >> 7) & 127


def coord_k(code):
    return (code >> 14) & 127


def present(code):
    return code >> PRESENT


def plan(owner_hbm, coords_hbm, code_ref, rounds_ref, owner_ref, coords_ref, sem, *, slots, rows_count, blocks):
    t = lax.axis_index("tiles")
    r = lax.axis_index("rows")
    tiles = owner_ref.shape[1]
    chips = rows_count // CORES
    shift = (blocks * CORES).bit_length() - 1
    loads = [
        pltpu.make_async_copy(owner_hbm, owner_ref, sem.at[0]),
        pltpu.make_async_copy(coords_hbm, coords_ref, sem.at[1]),
    ]
    for load in loads:
        load.start()
    for load in loads:
        load.wait()
    owner = owner_ref[...]
    coords = coords_ref[...]
    first, second, third = coords[0:1], coords[1:2], coords[2:3]
    code = first + (second << 7) + (third << 14) + (1 << PRESENT)
    key_b = owner * chips + (second >> shift)
    key_c = owner * chips + (third >> shift)
    lanes = jnp.concatenate([owner, code, key_b, key_c, owner, code, key_b, key_c], axis=0)
    columns = jnp.transpose(lanes)
    owner_at, code_at = columns[:, 0:1], columns[:, 1:2]
    key_b_at, key_c_at = columns[:, 2:3], columns[:, 3:4]
    square = (tiles, tiles)
    number_at = lax.broadcasted_iota(jnp.int32, square, 0)
    number = lax.broadcasted_iota(jnp.int32, square, 1)
    one = jnp.ones(square, jnp.int32)
    zero = jnp.zeros(square, jnp.int32)
    earlier = jnp.where((owner_at == owner) & (number < number_at), one, zero)
    slot_at = owner_at * slots + jnp.sum(earlier, axis=1, keepdims=True)
    place = lax.broadcasted_iota(jnp.int32, (1, LANES), 1)
    within = place % slots
    column = ((place // slots) * rows_count + r) * slots + within
    row = (t * rows_count + (place - 64) // slots) * slots + within
    wanted = jnp.where(place < 64, column, jnp.where(place < 96, row, -1))
    code_ref[...] = jnp.sum(jnp.where(slot_at == wanted, code_at, 0), axis=0, keepdims=True)
    most = jnp.zeros((1, 1), jnp.int32)
    for key_at in (key_b_at, key_c_at):
        same = jnp.where(key_at == key_b, one, zero) + jnp.where(key_at == key_c, one, zero)
        most = jnp.maximum(most, jnp.max(jnp.sum(same, axis=1, keepdims=True), axis=0, keepdims=True))
    rounds = jnp.zeros((1, 1), jnp.int32)
    base = 0
    for capacity in CAPACITIES[:-1]:
        base = base + capacity
        rounds = rounds + jnp.where(most > base, 1, 0)
    rounds_ref[0, 0] = jnp.sum(rounds)


def gather_factors(code_ref, fb_ref, fc_ref, sb_ref, sc_ref, *refs, slots):
    outs, sem = refs[:-1], refs[-1]
    r = lax.axis_index("rows")
    blocks = fb_ref.shape[0]
    count = jnp.int32(0)
    for x in range(outs[0].shape[0]):
        at = jnp.int32(0)
        for s in range(slots):
            code = code_ref[0, 64 + (x * CORES + r % CORES) * slots + s]
            for own, sibling, coord in ((fb_ref, sb_ref, coord_j(code)), (fc_ref, sc_ref, coord_k(code))):
                shard = coord // blocks
                hit = (present(code) > 0) & (shard // CORES == r // CORES)

                @pl.when(hit)
                def _(own=own, sibling=sibling, coord=coord, shard=shard, at=at, x=x, s=s):
                    base = 0
                    for out, capacity in zip(outs, CAPACITIES):
                        if base >= 2 * s + 2:
                            break
                        inside = (at >= base) & (at < base + capacity)
                        for ref, held in ((own, shard == r), (sibling, shard != r)):

                            @pl.when(inside & held)
                            def _(ref=ref, out=out, base=base):
                                pltpu.make_async_copy(
                                    ref.at[coord % blocks], out.at[x, at - base], sem
                                ).start()

                        base = base + capacity

                at = at + hit.astype(jnp.int32)
        count = count + at

    def drain(_, carry):
        pltpu.make_async_copy(fb_ref.at[0], outs[0].at[0, 0], sem).wait()
        return carry

    lax.fori_loop(0, count, drain, 0)


def chip_gram(fb_ref, fc_ref, sb_ref, sc_ref, out_ref, buf, sem):
    core = lax.axis_index("rows") % CORES
    over = (((0,), (0,)), ((), ()))
    for which, (own, sibling) in enumerate(((fb_ref, sb_ref), (fc_ref, sc_ref))):

        @pl.when(core == which)
        def _(own=own, sibling=sibling):
            copies = [
                pltpu.make_async_copy(ref, buf.at[at], sem.at[at])
                for at, ref in enumerate((own, sibling))
            ]
            for copy in copies:
                copy.start()
            for copy in copies:
                copy.wait()

    out_ref[...] = sum(
        lax.dot_general(buf[at], buf[at], over, preferred_element_type=F32) for at in range(CORES)
    )


def contract(code_ref, x_ref, *refs, slots, blocks):
    ins = refs[: len(CAPACITIES)]
    out_ref, buf, bs, cs, scalar_ref, code_sem, sem = refs[len(CAPACITIES) :]
    r = lax.axis_index("rows")
    edge = x_ref.shape[1]
    part = edge // PARTS

    def fetch(s, q):
        rows = pl.ds(q * part, part)
        return pltpu.make_async_copy(x_ref.at[s, rows], buf.at[s, rows], sem.at[s, q])

    codes_copy = pltpu.make_async_copy(code_ref, scalar_ref, code_sem)
    codes_copy.start()
    for s in range(slots):
        for q in range(PARTS):
            fetch(s, q).start()
    codes_copy.wait()
    codes = [scalar_ref[0, 64 + r * slots + s] for s in range(slots)]
    live = jnp.int32(0)
    for code in codes:
        live = live + present(code)
    chips = []
    for s, code in enumerate(codes):
        for coord, keep in ((coord_j(code), bs), (coord_k(code), cs)):
            chip = coord // (blocks * CORES)
            at = jnp.int32(0)
            for other in chips:
                at = at + (other == chip).astype(jnp.int32)
            chips.append(chip)
            at = jnp.where(present(code) > 0, at, 0)
            base = 0
            value = None
            for ref, capacity in zip(ins, CAPACITIES):
                if base >= 2 * s + 2:
                    break
                inside = (at >= base) & (at < base + capacity)
                held = ref[chip, jnp.where(inside, at - base, 0)].astype(F32)
                value = held if value is None else jnp.where(inside, held, value)
                base = base + capacity
            keep[s] = value.astype(keep.dtype)
    out_ref[...] = jnp.zeros_like(out_ref)

    def multiply(s, q):
        b = bs[s]
        c = cs[s]
        for a in range(q * part, (q + 1) * part, CHUNK):
            x = buf[s, a : a + CHUNK].reshape(CHUNK * edge, edge)
            inner = jnp.dot(x, c, preferred_element_type=F32).reshape(CHUNK, edge, edge)
            total = jnp.sum(inner * b[None], axis=1)
            for u in range(CHUNK // STRIP):
                out_ref[a // STRIP + u, s] = total[u * STRIP : (u + 1) * STRIP]

    def whole(s, carry):
        for q in range(PARTS):
            fetch(s, q).wait()
        for q in range(PARTS):
            multiply(s, q)
        return carry

    last = live - 1
    lax.fori_loop(0, last, whole, 0)

    @pl.when(live > 0)
    def _():
        for q in range(PARTS):
            fetch(last, q).wait()
            multiply(last, q)

    def drain(s, carry):
        for q in range(PARTS):
            fetch(s, q).wait()
        return carry

    lax.fori_loop(live, slots, drain, 0)


def eliminate(matrix):
    size = matrix.shape[0]
    down = lax.broadcasted_iota(jnp.int32, (size, size), 0)
    across = lax.broadcasted_iota(jnp.int32, (size, size), 1)
    eye = jnp.where(down == across, 1.0, 0.0).astype(F32)
    both = jnp.concatenate([matrix, eye], axis=1)
    wide = lax.broadcasted_iota(jnp.int32, both.shape, 0)

    def spread(x):
        return jnp.broadcast_to(x, (x.shape[0], both.shape[1]))

    def pair(p, q, r):
        over = 1.0 / p
        ratio = q * over
        low = 1.0 / (r - q * ratio)
        side = ratio * low
        return over + ratio * side, side, low, ratio

    for k in range(0, size, 4):
        top = k // STRIP * STRIP
        rest = both[top:]
        row = [both[k + i : k + i + 1] for i in range(4)]
        p = {(i, j): spread(row[i][:, k + j : k + j + 1]) for i in range(4) for j in range(i, 4)}
        col = [spread(rest[:, k + j : k + j + 1]) for j in range(4)]
        a, b, c, ratio = pair(p[0, 0], p[0, 1], p[1, 1])
        u0, u1 = a * row[0] - b * row[1], c * row[1] - b * row[0]
        u02, u12 = a * p[0, 2] - b * p[1, 2], c * p[1, 2] - b * p[0, 2]
        u03, u13 = a * p[0, 3] - b * p[1, 3], c * p[1, 3] - b * p[0, 3]
        row2 = row[2] - p[0, 2] * u0 - p[1, 2] * u1
        row3 = row[3] - p[0, 3] * u0 - p[1, 3] * u1
        s22 = p[2, 2] - p[0, 2] * u02 - p[1, 2] * u12
        s23 = p[2, 3] - p[0, 3] * u02 - p[1, 3] * u12
        s33 = p[3, 3] - p[0, 3] * u03 - p[1, 3] * u13
        a, b, c, ratio2 = pair(s22, s23, s33)
        u2, u3 = a * row2 - b * row3, c * row3 - b * row2
        v0 = u0 - u02 * u2 - u03 * u3
        v1 = u1 - u12 * u2 - u13 * u3
        at = wide[top:]
        later = rest - col[0] * v0 - col[1] * v1 - col[2] * u2 - col[3] * u3
        rest = jnp.where(at == k + 1, row[1] - ratio * row[0], rest)
        rest = jnp.where(at == k + 2, row2, rest)
        rest = jnp.where(at == k + 3, row3 - ratio2 * row2, rest)
        rest = jnp.where(at > k + 3, later, rest)
        both = rest if top == 0 else jnp.concatenate([both[:top], rest], axis=0)
    pivots = jnp.sum(jnp.where(down == across, both[:, :size], 0.0), axis=1, keepdims=True)
    return both[:, size:] * lax.rsqrt(pivots)


def times(a, b, over=((1,), (0,))):
    return lax.dot_general(a, b, (over, ((), ())), precision=HIGHEST, preferred_element_type=F32)


def invert(one_ref, other_ref, out_ref):
    normal = one_ref[...] * other_ref[...]
    half = normal.shape[0] // 2
    first = eliminate(normal[:half, :half])
    side = times(normal[half:, :half], first, ((1,), (1,)))
    second = eliminate(normal[half:, half:] - times(side, side, ((1,), (1,))))
    out_ref[:half, :half] = first
    out_ref[:half, half:] = jnp.zeros((half, half), F32)
    out_ref[half:, :half] = -times(second, times(side, first))
    out_ref[half:, half:] = second


def gather_blocks(code_ref, in_ref, out_ref, *, slots):
    out_ref[...] = jnp.zeros_like(out_ref)
    blocks = out_ref.shape[1]
    for d in range(in_ref.shape[0]):
        for s in range(slots):
            code = code_ref[0, d * slots + s]
            i = coord_i(code)
            value = jnp.where(present(code) > 0, in_ref[d, s], 0.0)
            out_ref[i // blocks, i % blocks] += value


def solve(in_ref, inv_ref, out_ref):
    total = in_ref[0]
    for q in range(1, in_ref.shape[0]):
        total = total + in_ref[q]
    blocks = total.shape[0]
    rows = total.reshape(blocks * STRIP, total.shape[2])
    inv = inv_ref[...]
    solved = times(times(rows, inv, ((1,), (1,))), inv).reshape(total.shape)
    largest = jnp.max(jnp.abs(solved), axis=2, keepdims=True)
    exponent = jnp.ceil(jnp.log2(jnp.maximum(largest, TINY)))
    scaled = solved * jnp.exp2(BITS - exponent)
    fixed = jnp.clip(jnp.round(scaled), 1 - FULL, FULL - 1).astype(jnp.int32).astype(jnp.int16)
    lane = lax.broadcasted_iota(jnp.int32, solved.shape[1:], 1)
    exponents = jnp.zeros(solved.shape[1:], F32)
    for b in range(blocks):
        exponents = jnp.where(lane == b, exponent[b], exponents)
    exponents = exponents.astype(jnp.int32).astype(jnp.int16)
    for d in range(out_ref.shape[0]):
        out_ref[d, :blocks] = fixed
        out_ref[d, blocks] = exponents


def unpack(in_ref, out_ref):
    blocks = out_ref.shape[0]
    for t in range(in_ref.shape[0]):
        scale = jnp.exp2(in_ref[t, blocks].astype(jnp.int32).astype(F32) - BITS)
        for b in range(blocks):
            out_ref[b, t] = in_ref[t, b].astype(jnp.int32).astype(F32) * scale[:, b : b + 1]


def body(tile_values, tile_coords, tile_owner, factor_b, factor_c):
    slots = tile_values.shape[0]
    edge = tile_values.shape[1]
    rank = factor_b.shape[1]
    shard = factor_b.shape[0]
    tiles_count = lax.axis_size("tiles")
    rows_count = lax.axis_size("rows")
    blocks = shard // edge
    tile = (STRIP, rank)

    chips = rows_count // CORES

    def from_peer(x, peer):
        return lax.ppermute(x, "rows", [(q, peer(q)) for q in range(rows_count)])

    def swap(x):
        groups = [[x * CORES + core for x in range(chips)] for core in range(CORES)]
        return lax.all_to_all(x, "rows", 0, 0, axis_index_groups=groups, tiled=True)

    sibling_b, sibling_c = (from_peer(f, lambda q: q ^ 1) for f in (factor_b, factor_c))
    codes, rounds = pl.pallas_call(
        lambda *refs: plan(*refs, slots=slots, rows_count=rows_count, blocks=blocks),
        name="plan",
        out_shape=(
            jax.ShapeDtypeStruct((1, LANES), jnp.int32),
            jax.ShapeDtypeStruct((1, 1), jnp.int32),
        ),
        in_specs=[pl.BlockSpec(memory_space=pltpu.HBM)] * 2,
        out_specs=(vmem(), smem()),
        scratch_shapes=[
            pltpu.VMEM((1, tile_owner.shape[0]), jnp.int32),
            pltpu.VMEM((3, tile_owner.shape[0]), jnp.int32),
            pltpu.SemaphoreType.DMA((2,)),
        ],
        compiler_params=LIMIT,
    )(in_hbm(tile_owner.reshape(1, -1)), in_hbm(tile_coords.T))
    by_block = lambda f: f.reshape(blocks, edge, rank)
    sent = pl.pallas_call(
        lambda *refs: gather_factors(*refs, slots=slots),
        name="gather_factors",
        out_shape=tuple(jax.ShapeDtypeStruct((chips, c, edge, rank), BF16) for c in CAPACITIES),
        in_specs=[smem()] + [hbm()] * 4,
        out_specs=(vmem(),) * len(CAPACITIES),
        scratch_shapes=[pltpu.SemaphoreType.DMA],
        compiler_params=LIMIT,
    )(
        codes,
        in_hbm(by_block(factor_b)),
        in_hbm(by_block(factor_c)),
        by_block(sibling_b),
        by_block(sibling_c),
    )
    rest = lax.cond(rounds[0, 0] > 0, swap, lambda x: x, sent[1])
    first, rest = lax.optimization_barrier((sent[0], rest))
    chosen = [swap(first), rest]
    own_b, own_c, sibling_b, sibling_c, *sent = lax.optimization_barrier(
        (factor_b, factor_c, sibling_b, sibling_c, *sent)
    )
    gram = pl.pallas_call(
        chip_gram,
        name="chip_gram",
        out_shape=jax.ShapeDtypeStruct((rank, rank), F32),
        in_specs=[hbm()] * 4,
        out_specs=vmem(),
        scratch_shapes=[
            pltpu.VMEM((CORES, shard, rank), BF16),
            pltpu.SemaphoreType.DMA((CORES,)),
        ],
        compiler_params=LIMIT,
        cost_estimate=SMALL,
    )(in_hbm(own_b), in_hbm(own_c), sibling_b, sibling_c)
    gram = gram + from_peer(gram, lambda q: q ^ CORES)
    chosen, gram = lax.optimization_barrier((chosen, gram))

    partials = pl.pallas_call(
        lambda *refs: contract(*refs, slots=slots, blocks=blocks),
        name="contract",
        out_shape=jax.ShapeDtypeStruct((tiles_count, slots) + tile, F32),
        in_specs=[vmem(), pl.BlockSpec(memory_space=pltpu.HBM)] + [vmem()] * len(CAPACITIES),
        out_specs=vmem(),
        scratch_shapes=[
            pltpu.VMEM(tile_values.shape, BF16),
            pltpu.VMEM((slots, edge, rank), F32),
            pltpu.VMEM((slots, edge, rank), BF16),
            pltpu.SMEM((1, LANES), jnp.int32),
            pltpu.SemaphoreType.DMA,
            pltpu.SemaphoreType.DMA((slots, PARTS)),
        ],
        compiler_params=pltpu.CompilerParams(vmem_limit_bytes=24 << 20),
        cost_estimate=pl.CostEstimate(flops=slots * 2 * edge**4, bytes_accessed=slots * 2 * edge**3, transcendentals=0),
    )(codes, in_hbm(tile_values), *chosen)
    moved = lax.all_to_all(partials, "tiles", 0, 0, tiled=True)
    gram = gram + from_peer(gram, lambda q: (chips - 1 - q // CORES) * CORES + q % CORES)
    moved, gram = lax.optimization_barrier((moved, gram))
    dense = pl.pallas_call(
        lambda *refs: gather_blocks(*refs, slots=slots),
        name="gather_blocks",
        out_shape=jax.ShapeDtypeStruct((rows_count, blocks) + tile, F32),
        in_specs=[smem(), vmem()],
        out_specs=vmem(),
        compiler_params=LIMIT,
    )(codes, moved)
    dense, gram = lax.optimization_barrier((dense, gram))
    other = from_peer(gram, lambda q: q ^ 1)
    owned = lax.all_to_all(dense, "rows", 0, 0, tiled=True)
    inverse = pl.pallas_call(
        invert,
        name="invert",
        out_shape=jax.ShapeDtypeStruct((rank, rank), F32),
        in_specs=[vmem()] * 2,
        out_specs=vmem(),
        compiler_params=LIMIT,
        cost_estimate=pl.CostEstimate(flops=1 << 30, bytes_accessed=1 << 20, transcendentals=64),
    )(gram, other)
    solved = pl.pallas_call(
        solve,
        name="solve",
        out_shape=jax.ShapeDtypeStruct((tiles_count, blocks + 1) + tile, jnp.int16),
        in_specs=[vmem(), vmem()],
        out_specs=vmem(),
        compiler_params=LIMIT,
    )(owned, inverse)
    full = lax.all_to_all(solved, "tiles", 0, 0, tiled=True)
    out = pl.pallas_call(
        unpack,
        name="unpack",
        out_shape=jax.ShapeDtypeStruct((blocks, tiles_count) + tile, F32),
        in_specs=[vmem()],
        out_specs=vmem(),
        compiler_params=LIMIT,
    )(full)
    return out.reshape(shard, rank)


def solution(mesh):
    in_specs = (P(("tiles", "rows"), None, None, None), P(), P(), P("rows", None), P("rows", None))
    out_specs = P("rows", None)
    return jax.shard_map(body, mesh=mesh, in_specs=in_specs, out_specs=out_specs, check_vma=False)
```

```python
import jax
import jax.numpy as jnp
from jax import lax
from jax.experimental import pallas as pl
from jax.experimental.pallas import tpu as pltpu
from jax.sharding import PartitionSpec as P

F32 = jnp.float32
BF16 = jnp.bfloat16
HIGHEST = lax.Precision.HIGHEST
STRIP = 8
PRESENT = 21
CHUNK = 16
PARTS = 4
LANES = 128
BITS = 15.0
FULL = 32768.0
TINY = 2.0**-111
CAPACITIES = (6, 2)
CORES = 2
SMALL = pl.CostEstimate(flops=1024, bytes_accessed=1024, transcendentals=0)
LIMIT = pltpu.CompilerParams(vmem_limit_bytes=8 << 20)


def vmem():
    return pl.BlockSpec(memory_space=pltpu.VMEM)


def smem():
    return pl.BlockSpec(memory_space=pltpu.SMEM)


def hbm():
    return pl.BlockSpec(memory_space=pl.ANY)


def in_hbm(x):
    return pltpu.with_memory_space_constraint(x, pltpu.HBM)


def coord_i(code):
    return code & 127


def coord_j(code):
    return (code >> 7) & 127


def coord_k(code):
    return (code >> 14) & 127


def present(code):
    return code >> PRESENT


def plan(
    owner_hbm, coords_hbm, fb_hbm, fc_hbm, code_ref, rounds_ref, fb_ref, fc_ref, owner_ref, coords_ref, sem,
    *, slots, rows_count, blocks
):
    t = lax.axis_index("tiles")
    r = lax.axis_index("rows")
    tiles = owner_ref.shape[1]
    chips = rows_count // CORES
    shift = (blocks * CORES).bit_length() - 1
    loads = [
        pltpu.make_async_copy(owner_hbm, owner_ref, sem.at[0]),
        pltpu.make_async_copy(coords_hbm, coords_ref, sem.at[1]),
    ]
    shards = [
        pltpu.make_async_copy(fb_hbm, fb_ref, sem.at[2]),
        pltpu.make_async_copy(fc_hbm, fc_ref, sem.at[3]),
    ]
    for load in loads + shards:
        load.start()
    for load in loads:
        load.wait()
    owner = owner_ref[...]
    coords = coords_ref[...]
    first, second, third = coords[0:1], coords[1:2], coords[2:3]
    code = first + (second << 7) + (third << 14) + (1 << PRESENT)
    key_b = owner * chips + (second >> shift)
    key_c = owner * chips + (third >> shift)
    lanes = jnp.concatenate([owner, code, key_b, key_c, owner, code, key_b, key_c], axis=0)
    columns = jnp.transpose(lanes)
    owner_at, code_at = columns[:, 0:1], columns[:, 1:2]
    key_b_at, key_c_at = columns[:, 2:3], columns[:, 3:4]
    square = (tiles, tiles)
    number_at = lax.broadcasted_iota(jnp.int32, square, 0)
    number = lax.broadcasted_iota(jnp.int32, square, 1)
    one = jnp.ones(square, jnp.int32)
    zero = jnp.zeros(square, jnp.int32)
    earlier = jnp.where((owner_at == owner) & (number < number_at), one, zero)
    slot_at = owner_at * slots + jnp.sum(earlier, axis=1, keepdims=True)
    place = lax.broadcasted_iota(jnp.int32, (1, LANES), 1)
    within = place % slots
    column = ((place // slots) * rows_count + r) * slots + within
    row = (t * rows_count + (place - 64) // slots) * slots + within
    wanted = jnp.where(place < 64, column, jnp.where(place < 96, row, -1))
    code_ref[...] = jnp.sum(jnp.where(slot_at == wanted, code_at, 0), axis=0, keepdims=True)
    most = jnp.zeros((1, 1), jnp.int32)
    for key_at in (key_b_at, key_c_at):
        same = jnp.where(key_at == key_b, one, zero) + jnp.where(key_at == key_c, one, zero)
        most = jnp.maximum(most, jnp.max(jnp.sum(same, axis=1, keepdims=True), axis=0, keepdims=True))
    rounds = jnp.zeros((1, 1), jnp.int32)
    base = 0
    for capacity in CAPACITIES[:-1]:
        base = base + capacity
        rounds = rounds + jnp.where(most > base, 1, 0)
    rounds_ref[0, 0] = jnp.sum(rounds)
    for load in shards:
        load.wait()


def gather_factors(code_ref, fb_ref, fc_ref, sb_ref, sc_ref, *refs, slots):
    outs, sem = refs[:-1], refs[-1]
    r = lax.axis_index("rows")
    blocks = fb_ref.shape[0]
    count = jnp.int32(0)
    for x in range(outs[0].shape[0]):
        at = jnp.int32(0)
        for s in range(slots):
            code = code_ref[0, 64 + (x * CORES + r % CORES) * slots + s]
            for own, sibling, coord in ((fb_ref, sb_ref, coord_j(code)), (fc_ref, sc_ref, coord_k(code))):
                shard = coord // blocks
                hit = (present(code) > 0) & (shard // CORES == r // CORES)

                @pl.when(hit)
                def _(own=own, sibling=sibling, coord=coord, shard=shard, at=at, x=x, s=s):
                    base = 0
                    for out, capacity in zip(outs, CAPACITIES):
                        if base >= 2 * s + 2:
                            break
                        inside = (at >= base) & (at < base + capacity)
                        for ref, held in ((own, shard == r), (sibling, shard != r)):

                            @pl.when(inside & held)
                            def _(ref=ref, out=out, base=base):
                                pltpu.make_async_copy(
                                    ref.at[coord % blocks], out.at[x, at - base], sem
                                ).start()

                        base = base + capacity

                at = at + hit.astype(jnp.int32)
        count = count + at

    def drain(_, carry):
        pltpu.make_async_copy(fb_ref.at[0], outs[0].at[0, 0], sem).wait()
        return carry

    lax.fori_loop(0, count, drain, 0)


def chip_gram(fb_ref, fc_ref, sb_ref, sc_ref, out_ref, buf, sem):
    core = lax.axis_index("rows") % CORES
    over = (((0,), (0,)), ((), ()))
    for which, (own, sibling) in enumerate(((fb_ref, sb_ref), (fc_ref, sc_ref))):

        @pl.when(core == which)
        def _(own=own, sibling=sibling):
            copies = [
                pltpu.make_async_copy(ref, buf.at[at], sem.at[at])
                for at, ref in enumerate((own, sibling))
            ]
            for copy in copies:
                copy.start()
            for copy in copies:
                copy.wait()

    out_ref[...] = sum(
        lax.dot_general(buf[at], buf[at], over, preferred_element_type=F32) for at in range(CORES)
    )


def load_part(x_ref, out_ref, sem):
    copy = pltpu.make_async_copy(x_ref.at[0, pl.ds(0, out_ref.shape[0])], out_ref, sem)
    copy.start()
    copy.wait()


def contract(code_ref, x_ref, part_ref, *refs, slots, blocks):
    ins = refs[: len(CAPACITIES)]
    out_ref, buf, bs, cs, scalar_ref, code_sem, sem = refs[len(CAPACITIES) :]
    r = lax.axis_index("rows")
    edge = x_ref.shape[1]
    part = edge // PARTS

    def fetch(s, q):
        rows = pl.ds(q * part, part)
        return pltpu.make_async_copy(x_ref.at[s, rows], buf.at[s, rows], sem.at[s, q])

    codes_copy = pltpu.make_async_copy(code_ref, scalar_ref, code_sem)
    codes_copy.start()
    early = part_ref.shape[0] // part
    for q in range(early):
        rows = pl.ds(q * part, part)
        pltpu.make_async_copy(part_ref.at[rows], buf.at[0, rows], sem.at[0, q]).start()
    for s in range(slots):
        for q in range(early if s == 0 else 0, PARTS):
            fetch(s, q).start()
    codes_copy.wait()
    codes = [scalar_ref[0, 64 + r * slots + s] for s in range(slots)]
    live = jnp.int32(0)
    for code in codes:
        live = live + present(code)
    chips = []
    for s, code in enumerate(codes):
        for coord, keep in ((coord_j(code), bs), (coord_k(code), cs)):
            chip = coord // (blocks * CORES)
            at = jnp.int32(0)
            for other in chips:
                at = at + (other == chip).astype(jnp.int32)
            chips.append(chip)
            at = jnp.where(present(code) > 0, at, 0)
            base = 0
            value = None
            for ref, capacity in zip(ins, CAPACITIES):
                if base >= 2 * s + 2:
                    break
                inside = (at >= base) & (at < base + capacity)
                held = ref[chip, jnp.where(inside, at - base, 0)].astype(F32)
                value = held if value is None else jnp.where(inside, held, value)
                base = base + capacity
            keep[s] = value.astype(keep.dtype)
    out_ref[...] = jnp.zeros_like(out_ref)

    def multiply(s, q):
        b = bs[s]
        c = cs[s]
        for a in range(q * part, (q + 1) * part, CHUNK):
            x = buf[s, a : a + CHUNK].reshape(CHUNK * edge, edge)
            inner = jnp.dot(x, c, preferred_element_type=F32).reshape(CHUNK, edge, edge)
            total = jnp.sum(inner * b[None], axis=1)
            for u in range(CHUNK // STRIP):
                out_ref[a // STRIP + u, s] = total[u * STRIP : (u + 1) * STRIP]

    def whole(s, carry):
        for q in range(PARTS):
            fetch(s, q).wait()
        for q in range(PARTS):
            multiply(s, q)
        return carry

    last = live - 1
    lax.fori_loop(0, last, whole, 0)

    @pl.when(live > 0)
    def _():
        for q in range(PARTS):
            fetch(last, q).wait()
            multiply(last, q)

    def drain(s, carry):
        for q in range(PARTS):
            fetch(s, q).wait()
        return carry

    lax.fori_loop(live, slots, drain, 0)


def eliminate(matrix):
    size = matrix.shape[0]
    down = lax.broadcasted_iota(jnp.int32, (size, size), 0)
    across = lax.broadcasted_iota(jnp.int32, (size, size), 1)
    eye = jnp.where(down == across, 1.0, 0.0).astype(F32)
    both = jnp.concatenate([matrix, eye], axis=1)
    wide = lax.broadcasted_iota(jnp.int32, both.shape, 0)

    def spread(x):
        return jnp.broadcast_to(x, (x.shape[0], both.shape[1]))

    def pair(p, q, r):
        over = 1.0 / p
        ratio = q * over
        low = 1.0 / (r - q * ratio)
        side = ratio * low
        return over + ratio * side, side, low, ratio

    for k in range(0, size, 4):
        top = k // STRIP * STRIP
        rest = both[top:]
        row = [both[k + i : k + i + 1] for i in range(4)]
        p = {(i, j): spread(row[i][:, k + j : k + j + 1]) for i in range(4) for j in range(i, 4)}
        col = [spread(rest[:, k + j : k + j + 1]) for j in range(4)]
        a, b, c, ratio = pair(p[0, 0], p[0, 1], p[1, 1])
        u0, u1 = a * row[0] - b * row[1], c * row[1] - b * row[0]
        u02, u12 = a * p[0, 2] - b * p[1, 2], c * p[1, 2] - b * p[0, 2]
        u03, u13 = a * p[0, 3] - b * p[1, 3], c * p[1, 3] - b * p[0, 3]
        row2 = row[2] - p[0, 2] * u0 - p[1, 2] * u1
        row3 = row[3] - p[0, 3] * u0 - p[1, 3] * u1
        s22 = p[2, 2] - p[0, 2] * u02 - p[1, 2] * u12
        s23 = p[2, 3] - p[0, 3] * u02 - p[1, 3] * u12
        s33 = p[3, 3] - p[0, 3] * u03 - p[1, 3] * u13
        a, b, c, ratio2 = pair(s22, s23, s33)
        u2, u3 = a * row2 - b * row3, c * row3 - b * row2
        v0 = u0 - u02 * u2 - u03 * u3
        v1 = u1 - u12 * u2 - u13 * u3
        at = wide[top:]
        later = rest - col[0] * v0 - col[1] * v1 - col[2] * u2 - col[3] * u3
        rest = jnp.where(at == k + 1, row[1] - ratio * row[0], rest)
        rest = jnp.where(at == k + 2, row2, rest)
        rest = jnp.where(at == k + 3, row3 - ratio2 * row2, rest)
        rest = jnp.where(at > k + 3, later, rest)
        both = rest if top == 0 else jnp.concatenate([both[:top], rest], axis=0)
    pivots = jnp.sum(jnp.where(down == across, both[:, :size], 0.0), axis=1, keepdims=True)
    return both[:, size:] * lax.rsqrt(pivots)


def times(a, b, over=((1,), (0,))):
    return lax.dot_general(a, b, (over, ((), ())), precision=HIGHEST, preferred_element_type=F32)


def invert(one_ref, other_ref, out_ref):
    normal = one_ref[...] * other_ref[...]
    half = normal.shape[0] // 2
    first = eliminate(normal[:half, :half])
    side = times(normal[half:, :half], first, ((1,), (1,)))
    second = eliminate(normal[half:, half:] - times(side, side, ((1,), (1,))))
    out_ref[:half, :half] = first
    out_ref[:half, half:] = jnp.zeros((half, half), F32)
    out_ref[half:, :half] = -times(second, times(side, first))
    out_ref[half:, half:] = second


def gather_blocks(code_ref, in_ref, keep_ref, send_ref, both, *, slots):
    core = lax.axis_index("rows") % CORES
    blocks = both.shape[2]
    both[...] = jnp.zeros_like(both)
    for d in range(in_ref.shape[0]):
        for s in range(slots):
            code = code_ref[0, d * slots + s]
            i = coord_i(code)
            shard = i // blocks
            value = jnp.where(present(code) > 0, in_ref[d, s], 0.0)
            both[(shard + core) % CORES, shard // CORES, i % blocks] += value
    keep_ref[...] = both[0]
    send_ref[...] = both[1]


def solve(in_ref, inv_ref, out_ref):
    total = in_ref[0]
    for q in range(1, in_ref.shape[0]):
        total = total + in_ref[q]
    blocks = total.shape[0]
    rows = total.reshape(blocks * STRIP, total.shape[2])
    inv = inv_ref[...]
    solved = times(times(rows, inv, ((1,), (1,))), inv).reshape(total.shape)
    largest = jnp.max(jnp.abs(solved), axis=2, keepdims=True)
    exponent = jnp.ceil(jnp.log2(jnp.maximum(largest, TINY)))
    scaled = solved * jnp.exp2(BITS - exponent)
    fixed = jnp.clip(jnp.round(scaled), 1 - FULL, FULL - 1).astype(jnp.int32).astype(jnp.int16)
    lane = lax.broadcasted_iota(jnp.int32, solved.shape[1:], 1)
    exponents = jnp.zeros(solved.shape[1:], F32)
    for b in range(blocks):
        exponents = jnp.where(lane == b, exponent[b], exponents)
    exponents = exponents.astype(jnp.int32).astype(jnp.int16)
    for d in range(out_ref.shape[0]):
        out_ref[d, :blocks] = fixed
        out_ref[d, blocks] = exponents


def unpack(in_ref, out_ref, buf, sem):
    blocks = out_ref.shape[0]
    group = blocks // sem.shape[0]
    scales = []
    for t in range(in_ref.shape[0]):
        scales.append(jnp.exp2(in_ref[t, blocks].astype(jnp.int32).astype(F32) - BITS))
    copies = []
    for g in range(sem.shape[0]):
        for b in range(g * group, (g + 1) * group):
            for t, scale in enumerate(scales):
                buf[b, t] = in_ref[t, b].astype(jnp.int32).astype(F32) * scale[:, b : b + 1]
        part = pl.ds(g * group, group)
        copies.append(pltpu.make_async_copy(buf.at[part], out_ref.at[part], sem.at[g]))
        copies[-1].start()
    for copy in copies:
        copy.wait()


def body(tile_values, tile_coords, tile_owner, factor_b, factor_c):
    slots = tile_values.shape[0]
    edge = tile_values.shape[1]
    rank = factor_b.shape[1]
    shard = factor_b.shape[0]
    tiles_count = lax.axis_size("tiles")
    rows_count = lax.axis_size("rows")
    blocks = shard // edge
    tile = (STRIP, rank)

    chips = rows_count // CORES

    def from_peer(x, peer):
        return lax.ppermute(x, "rows", [(q, peer(q)) for q in range(rows_count)])

    def swap(x):
        groups = [[x * CORES + core for x in range(chips)] for core in range(CORES)]
        return lax.all_to_all(x, "rows", 0, 0, axis_index_groups=groups, tiled=True)

    sibling_b, sibling_c = (from_peer(f, lambda q: q ^ 1) for f in (factor_b, factor_c))
    by_block = lambda f: f.reshape(blocks, edge, rank)
    shards = jax.ShapeDtypeStruct((blocks, edge, rank), BF16)
    codes, rounds, shard_b, shard_c = pl.pallas_call(
        lambda *refs: plan(*refs, slots=slots, rows_count=rows_count, blocks=blocks),
        name="plan",
        out_shape=(
            jax.ShapeDtypeStruct((1, LANES), jnp.int32),
            jax.ShapeDtypeStruct((1, 1), jnp.int32),
            shards,
            shards,
        ),
        in_specs=[pl.BlockSpec(memory_space=pltpu.HBM)] * 4,
        out_specs=(vmem(), smem(), vmem(), vmem()),
        scratch_shapes=[
            pltpu.VMEM((1, tile_owner.shape[0]), jnp.int32),
            pltpu.VMEM((3, tile_owner.shape[0]), jnp.int32),
            pltpu.SemaphoreType.DMA((4,)),
        ],
        compiler_params=LIMIT,
    )(
        in_hbm(tile_owner.reshape(1, -1)),
        in_hbm(tile_coords.T),
        in_hbm(by_block(factor_b)),
        in_hbm(by_block(factor_c)),
    )
    sent = pl.pallas_call(
        lambda *refs: gather_factors(*refs, slots=slots),
        name="gather_factors",
        out_shape=tuple(jax.ShapeDtypeStruct((chips, c, edge, rank), BF16) for c in CAPACITIES),
        in_specs=[smem()] + [hbm()] * 4,
        out_specs=(pl.BlockSpec(memory_space=pltpu.HBM),) * len(CAPACITIES),
        scratch_shapes=[pltpu.SemaphoreType.DMA],
        compiler_params=LIMIT,
    )(
        codes,
        shard_b,
        shard_c,
        by_block(sibling_b),
        by_block(sibling_c),
    )
    rest = lax.cond(rounds[0, 0] > 0, swap, lambda x: x, sent[1])
    first, rest = lax.optimization_barrier((sent[0], rest))
    chosen = [swap(first), rest]
    own_x, own_b, own_c, sibling_b, sibling_c, *sent = lax.optimization_barrier(
        (tile_values, factor_b, factor_c, sibling_b, sibling_c, *sent)
    )
    gram = pl.pallas_call(
        chip_gram,
        name="chip_gram",
        out_shape=jax.ShapeDtypeStruct((rank, rank), F32),
        in_specs=[hbm()] * 4,
        out_specs=vmem(),
        scratch_shapes=[
            pltpu.VMEM((CORES, shard, rank), BF16),
            pltpu.SemaphoreType.DMA((CORES,)),
        ],
        compiler_params=LIMIT,
        cost_estimate=SMALL,
    )(in_hbm(own_b), in_hbm(own_c), sibling_b, sibling_c)
    gram = gram + from_peer(gram, lambda q: q ^ CORES)
    part = pl.pallas_call(
        load_part,
        name="load_part",
        out_shape=jax.ShapeDtypeStruct((edge // 2, edge, edge), BF16),
        in_specs=[pl.BlockSpec(memory_space=pltpu.HBM)],
        out_specs=vmem(),
        scratch_shapes=[pltpu.SemaphoreType.DMA],
        compiler_params=LIMIT,
        cost_estimate=SMALL,
    )(in_hbm(own_x))
    chosen, gram = lax.optimization_barrier((chosen, gram))

    partials = pl.pallas_call(
        lambda *refs: contract(*refs, slots=slots, blocks=blocks),
        name="contract",
        out_shape=jax.ShapeDtypeStruct((tiles_count, slots) + tile, F32),
        in_specs=[vmem(), pl.BlockSpec(memory_space=pltpu.HBM), vmem()] + [vmem()] * len(CAPACITIES),
        out_specs=vmem(),
        scratch_shapes=[
            pltpu.VMEM(tile_values.shape, BF16),
            pltpu.VMEM((slots, edge, rank), F32),
            pltpu.VMEM((slots, edge, rank), BF16),
            pltpu.SMEM((1, LANES), jnp.int32),
            pltpu.SemaphoreType.DMA,
            pltpu.SemaphoreType.DMA((slots, PARTS)),
        ],
        compiler_params=pltpu.CompilerParams(vmem_limit_bytes=24 << 20),
        cost_estimate=pl.CostEstimate(flops=slots * 2 * edge**4, bytes_accessed=slots * 2 * edge**3, transcendentals=0),
    )(codes, in_hbm(tile_values), part, *chosen)
    moved = lax.all_to_all(partials, "tiles", 0, 0, tiled=True)
    gram = gram + from_peer(gram, lambda q: (chips - 1 - q // CORES) * CORES + q % CORES)
    moved, gram = lax.optimization_barrier((moved, gram))
    sums = jax.ShapeDtypeStruct((chips, blocks) + tile, F32)
    keep, send = pl.pallas_call(
        lambda *refs: gather_blocks(*refs, slots=slots),
        name="gather_blocks",
        out_shape=(sums, sums),
        in_specs=[smem(), vmem()],
        out_specs=(vmem(), vmem()),
        scratch_shapes=[pltpu.VMEM((CORES, chips, blocks) + tile, F32)],
        compiler_params=LIMIT,
    )(codes, moved)
    send, gram = lax.optimization_barrier((send, gram))
    other = from_peer(gram, lambda q: q ^ 1)
    summed, other = lax.optimization_barrier((keep + from_peer(send, lambda q: q ^ 1), other))
    owned = swap(summed)
    inverse = pl.pallas_call(
        invert,
        name="invert",
        out_shape=jax.ShapeDtypeStruct((rank, rank), F32),
        in_specs=[vmem()] * 2,
        out_specs=vmem(),
        compiler_params=LIMIT,
        cost_estimate=pl.CostEstimate(flops=1 << 30, bytes_accessed=1 << 20, transcendentals=64),
    )(gram, other)
    solved = pl.pallas_call(
        solve,
        name="solve",
        out_shape=jax.ShapeDtypeStruct((tiles_count, blocks + 1) + tile, jnp.int16),
        in_specs=[vmem(), vmem()],
        out_specs=vmem(),
        compiler_params=LIMIT,
    )(owned, inverse)
    full = lax.all_to_all(solved, "tiles", 0, 0, tiled=True)
    out = pl.pallas_call(
        unpack,
        name="unpack",
        out_shape=jax.ShapeDtypeStruct((blocks, tiles_count) + tile, F32),
        in_specs=[vmem()],
        out_specs=pl.BlockSpec(memory_space=pltpu.HBM),
        scratch_shapes=[
            pltpu.VMEM((blocks, tiles_count) + tile, F32),
            pltpu.SemaphoreType.DMA((4,)),
        ],
        compiler_params=LIMIT,
    )(full)
    return out.reshape(shard, rank)


def solution(mesh):
    in_specs = (P(("tiles", "rows"), None, None, None), P(), P(), P("rows", None), P("rows", None))
    out_specs = P("rows", None)
    return jax.shard_map(body, mesh=mesh, in_specs=in_specs, out_specs=out_specs, check_vma=False)
```

```python
import jax
import jax.numpy as jnp
from jax import lax
from jax.experimental import pallas as pl
from jax.experimental.pallas import tpu as pltpu
from jax.sharding import PartitionSpec as P

F32 = jnp.float32
BF16 = jnp.bfloat16
HIGHEST = lax.Precision.HIGHEST
STRIP = 8
PRESENT = 21
CHUNK = 16
PARTS = 4
LANES = 128
BITS = 15.0
FULL = 32768.0
TINY = 2.0**-111
CAPACITIES = (6, 2)
CORES = 2
SMALL = pl.CostEstimate(flops=1024, bytes_accessed=1024, transcendentals=0)
LIMIT = pltpu.CompilerParams(vmem_limit_bytes=8 << 20)


def vmem():
    return pl.BlockSpec(memory_space=pltpu.VMEM)


def smem():
    return pl.BlockSpec(memory_space=pltpu.SMEM)


def hbm():
    return pl.BlockSpec(memory_space=pl.ANY)


def in_hbm(x):
    return pltpu.with_memory_space_constraint(x, pltpu.HBM)


def coord_i(code):
    return code & 127


def coord_j(code):
    return (code >> 7) & 127


def coord_k(code):
    return (code >> 14) & 127


def present(code):
    return code >> PRESENT


def plan(
    owner_hbm, coords_hbm, fb_hbm, fc_hbm, code_ref, rounds_ref, fb_ref, fc_ref, owner_ref, coords_ref, sem,
    *, slots, rows_count, blocks
):
    t = lax.axis_index("tiles")
    r = lax.axis_index("rows")
    tiles = owner_ref.shape[1]
    chips = rows_count // CORES
    shift = (blocks * CORES).bit_length() - 1
    loads = [
        pltpu.make_async_copy(owner_hbm, owner_ref, sem.at[0]),
        pltpu.make_async_copy(coords_hbm, coords_ref, sem.at[1]),
    ]
    shards = [
        pltpu.make_async_copy(fb_hbm, fb_ref, sem.at[2]),
        pltpu.make_async_copy(fc_hbm, fc_ref, sem.at[3]),
    ]
    for load in loads + shards:
        load.start()
    for load in loads:
        load.wait()
    owner = owner_ref[...]
    coords = coords_ref[...]
    first, second, third = coords[0:1], coords[1:2], coords[2:3]
    code = first + (second << 7) + (third << 14) + (1 << PRESENT)
    key_b = owner * chips + (second >> shift)
    key_c = owner * chips + (third >> shift)
    lanes = jnp.concatenate([owner, code, key_b, key_c, owner, code, key_b, key_c], axis=0)
    columns = jnp.transpose(lanes)
    owner_at, code_at = columns[:, 0:1], columns[:, 1:2]
    key_b_at, key_c_at = columns[:, 2:3], columns[:, 3:4]
    square = (tiles, tiles)
    number_at = lax.broadcasted_iota(jnp.int32, square, 0)
    number = lax.broadcasted_iota(jnp.int32, square, 1)
    one = jnp.ones(square, jnp.int32)
    zero = jnp.zeros(square, jnp.int32)
    earlier = jnp.where((owner_at == owner) & (number < number_at), one, zero)
    slot_at = owner_at * slots + jnp.sum(earlier, axis=1, keepdims=True)
    place = lax.broadcasted_iota(jnp.int32, (1, LANES), 1)
    within = place % slots
    column = ((place // slots) * rows_count + r) * slots + within
    row = (t * rows_count + (place - 64) // slots) * slots + within
    wanted = jnp.where(place < 64, column, jnp.where(place < 96, row, -1))
    code_ref[...] = jnp.sum(jnp.where(slot_at == wanted, code_at, 0), axis=0, keepdims=True)
    most = jnp.zeros((1, 1), jnp.int32)
    for key_at in (key_b_at, key_c_at):
        same = jnp.where(key_at == key_b, one, zero) + jnp.where(key_at == key_c, one, zero)
        most = jnp.maximum(most, jnp.max(jnp.sum(same, axis=1, keepdims=True), axis=0, keepdims=True))
    rounds = jnp.zeros((1, 1), jnp.int32)
    base = 0
    for capacity in CAPACITIES[:-1]:
        base = base + capacity
        rounds = rounds + jnp.where(most > base, 1, 0)
    rounds_ref[0, 0] = jnp.sum(rounds)
    for load in shards:
        load.wait()


def gather_factors(code_ref, fb_ref, fc_ref, sb_ref, sc_ref, *refs, slots):
    outs, sem = refs[:-1], refs[-1]
    r = lax.axis_index("rows")
    blocks = fb_ref.shape[0]
    count = jnp.int32(0)
    for x in range(outs[0].shape[0]):
        at = jnp.int32(0)
        for s in range(slots):
            code = code_ref[0, 64 + (x * CORES + r % CORES) * slots + s]
            for own, sibling, coord in ((fb_ref, sb_ref, coord_j(code)), (fc_ref, sc_ref, coord_k(code))):
                shard = coord // blocks
                hit = (present(code) > 0) & (shard // CORES == r // CORES)

                @pl.when(hit)
                def _(own=own, sibling=sibling, coord=coord, shard=shard, at=at, x=x, s=s):
                    base = 0
                    for out, capacity in zip(outs, CAPACITIES):
                        if base >= 2 * s + 2:
                            break
                        inside = (at >= base) & (at < base + capacity)
                        for ref, held in ((own, shard == r), (sibling, shard != r)):

                            @pl.when(inside & held)
                            def _(ref=ref, out=out, base=base):
                                pltpu.make_async_copy(
                                    ref.at[coord % blocks], out.at[x, at - base], sem
                                ).start()

                        base = base + capacity

                at = at + hit.astype(jnp.int32)
        count = count + at

    def drain(_, carry):
        pltpu.make_async_copy(fb_ref.at[0], outs[0].at[0, 0], sem).wait()
        return carry

    lax.fori_loop(0, count, drain, 0)


def chip_gram(fb_ref, fc_ref, sb_ref, sc_ref, out_ref, buf, sem):
    core = lax.axis_index("rows") % CORES
    over = (((0,), (0,)), ((), ()))
    for which, (own, sibling) in enumerate(((fb_ref, sb_ref), (fc_ref, sc_ref))):

        @pl.when(core == which)
        def _(own=own, sibling=sibling):
            copies = [
                pltpu.make_async_copy(ref, buf.at[at], sem.at[at])
                for at, ref in enumerate((own, sibling))
            ]
            for copy in copies:
                copy.start()
            for copy in copies:
                copy.wait()

    out_ref[...] = sum(
        lax.dot_general(buf[at], buf[at], over, preferred_element_type=F32) for at in range(CORES)
    )


def load_part(x_ref, out_ref, sem):
    copy = pltpu.make_async_copy(x_ref.at[0, pl.ds(0, out_ref.shape[0])], out_ref, sem)
    copy.start()
    copy.wait()


def contract(code_ref, x_ref, part_ref, *refs, slots, blocks):
    ins = refs[: len(CAPACITIES)]
    out_hbm, out_ref, buf, bs, cs, scalar_ref, code_sem, sem, out_sem = refs[len(CAPACITIES) :]
    r = lax.axis_index("rows")
    edge = x_ref.shape[1]
    part = edge // PARTS

    def fetch(s, q):
        rows = pl.ds(q * part, part)
        return pltpu.make_async_copy(x_ref.at[s, rows], buf.at[s, rows], sem.at[s, q])

    codes_copy = pltpu.make_async_copy(code_ref, scalar_ref, code_sem)
    codes_copy.start()
    early = part_ref.shape[0] // part
    for q in range(early):
        rows = pl.ds(q * part, part)
        pltpu.make_async_copy(part_ref.at[rows], buf.at[0, rows], sem.at[0, q]).start()
    for s in range(slots):
        for q in range(early if s == 0 else 0, PARTS):
            fetch(s, q).start()
    codes_copy.wait()
    codes = [scalar_ref[0, 64 + r * slots + s] for s in range(slots)]
    live = jnp.int32(0)
    for code in codes:
        live = live + present(code)
    chips = []
    for s, code in enumerate(codes):
        for coord, keep in ((coord_j(code), bs), (coord_k(code), cs)):
            chip = coord // (blocks * CORES)
            at = jnp.int32(0)
            for other in chips:
                at = at + (other == chip).astype(jnp.int32)
            chips.append(chip)
            at = jnp.where(present(code) > 0, at, 0)
            base = 0
            value = None
            for ref, capacity in zip(ins, CAPACITIES):
                if base >= 2 * s + 2:
                    break
                inside = (at >= base) & (at < base + capacity)
                held = ref[chip, jnp.where(inside, at - base, 0)].astype(F32)
                value = held if value is None else jnp.where(inside, held, value)
                base = base + capacity
            keep[s] = value.astype(keep.dtype)
    def store(s):
        return pltpu.make_async_copy(out_ref.at[:, s], out_hbm.at[:, s], out_sem.at[s])

    out_ref[...] = jnp.zeros_like(out_ref)
    for s in range(slots):

        @pl.when(s >= live)
        def _(s=s):
            store(s).start()

    def multiply(s, q):
        b = bs[s]
        c = cs[s]
        for a in range(q * part, (q + 1) * part, CHUNK):
            x = buf[s, a : a + CHUNK].reshape(CHUNK * edge, edge)
            inner = jnp.dot(x, c, preferred_element_type=F32).reshape(CHUNK, edge, edge)
            total = jnp.sum(inner * b[None], axis=1)
            for u in range(CHUNK // STRIP):
                out_ref[a // STRIP + u, s] = total[u * STRIP : (u + 1) * STRIP]

    def whole(s, carry):
        for q in range(PARTS):
            fetch(s, q).wait()
        for q in range(PARTS):
            multiply(s, q)
        store(s).start()
        return carry

    last = live - 1
    lax.fori_loop(0, last, whole, 0)

    @pl.when(live > 0)
    def _():
        for q in range(PARTS):
            fetch(last, q).wait()
            multiply(last, q)
        store(last).start()

    def drain(s, carry):
        for q in range(PARTS):
            fetch(s, q).wait()
        return carry

    lax.fori_loop(live, slots, drain, 0)
    for s in range(slots):
        store(s).wait()


def eliminate(matrix):
    size = matrix.shape[0]
    down = lax.broadcasted_iota(jnp.int32, (size, size), 0)
    across = lax.broadcasted_iota(jnp.int32, (size, size), 1)
    eye = jnp.where(down == across, 1.0, 0.0).astype(F32)
    both = jnp.concatenate([matrix, eye], axis=1)
    wide = lax.broadcasted_iota(jnp.int32, both.shape, 0)

    def spread(x):
        return jnp.broadcast_to(x, (x.shape[0], both.shape[1]))

    def pair(p, q, r):
        over = 1.0 / p
        ratio = q * over
        low = 1.0 / (r - q * ratio)
        side = ratio * low
        return over + ratio * side, side, low, ratio

    for k in range(0, size, 4):
        top = k // STRIP * STRIP
        rest = both[top:]
        row = [both[k + i : k + i + 1] for i in range(4)]
        p = {(i, j): spread(row[i][:, k + j : k + j + 1]) for i in range(4) for j in range(i, 4)}
        col = [spread(rest[:, k + j : k + j + 1]) for j in range(4)]
        a, b, c, ratio = pair(p[0, 0], p[0, 1], p[1, 1])
        u0, u1 = a * row[0] - b * row[1], c * row[1] - b * row[0]
        u02, u12 = a * p[0, 2] - b * p[1, 2], c * p[1, 2] - b * p[0, 2]
        u03, u13 = a * p[0, 3] - b * p[1, 3], c * p[1, 3] - b * p[0, 3]
        row2 = row[2] - p[0, 2] * u0 - p[1, 2] * u1
        row3 = row[3] - p[0, 3] * u0 - p[1, 3] * u1
        s22 = p[2, 2] - p[0, 2] * u02 - p[1, 2] * u12
        s23 = p[2, 3] - p[0, 3] * u02 - p[1, 3] * u12
        s33 = p[3, 3] - p[0, 3] * u03 - p[1, 3] * u13
        a, b, c, ratio2 = pair(s22, s23, s33)
        u2, u3 = a * row2 - b * row3, c * row3 - b * row2
        v0 = u0 - u02 * u2 - u03 * u3
        v1 = u1 - u12 * u2 - u13 * u3
        at = wide[top:]
        later = rest - col[0] * v0 - col[1] * v1 - col[2] * u2 - col[3] * u3
        rest = jnp.where(at == k + 1, row[1] - ratio * row[0], rest)
        rest = jnp.where(at == k + 2, row2, rest)
        rest = jnp.where(at == k + 3, row3 - ratio2 * row2, rest)
        rest = jnp.where(at > k + 3, later, rest)
        both = rest if top == 0 else jnp.concatenate([both[:top], rest], axis=0)
    pivots = jnp.sum(jnp.where(down == across, both[:, :size], 0.0), axis=1, keepdims=True)
    return both[:, size:] * lax.rsqrt(pivots)


def times(a, b, over=((1,), (0,))):
    return lax.dot_general(a, b, (over, ((), ())), precision=HIGHEST, preferred_element_type=F32)


def invert(one_ref, other_ref, out_ref):
    normal = one_ref[...] * other_ref[...]
    half = normal.shape[0] // 2
    first = eliminate(normal[:half, :half])
    side = times(normal[half:, :half], first, ((1,), (1,)))
    second = eliminate(normal[half:, half:] - times(side, side, ((1,), (1,))))
    out_ref[:half, :half] = first
    out_ref[:half, half:] = jnp.zeros((half, half), F32)
    out_ref[half:, :half] = -times(second, times(side, first))
    out_ref[half:, half:] = second


def gather_blocks(code_ref, in_ref, keep_ref, send_ref, both, *, slots):
    core = lax.axis_index("rows") % CORES
    blocks = both.shape[2]
    both[...] = jnp.zeros_like(both)
    for d in range(in_ref.shape[0]):
        for s in range(slots):
            code = code_ref[0, d * slots + s]
            i = coord_i(code)
            shard = i // blocks
            value = jnp.where(present(code) > 0, in_ref[d, s], 0.0)
            both[(shard + core) % CORES, shard // CORES, i % blocks] += value
    keep_ref[...] = both[0]
    send_ref[...] = both[1]


def solve(in_ref, inv_ref, out_ref):
    total = in_ref[0]
    for q in range(1, in_ref.shape[0]):
        total = total + in_ref[q]
    blocks = total.shape[0]
    rows = total.reshape(blocks * STRIP, total.shape[2])
    inv = inv_ref[...]
    solved = times(times(rows, inv, ((1,), (1,))), inv).reshape(total.shape)
    largest = jnp.max(jnp.abs(solved), axis=2, keepdims=True)
    exponent = jnp.ceil(jnp.log2(jnp.maximum(largest, TINY)))
    scaled = solved * jnp.exp2(BITS - exponent)
    fixed = jnp.clip(jnp.round(scaled), 1 - FULL, FULL - 1).astype(jnp.int32).astype(jnp.int16)
    lane = lax.broadcasted_iota(jnp.int32, solved.shape[1:], 1)
    exponents = jnp.zeros(solved.shape[1:], F32)
    for b in range(blocks):
        exponents = jnp.where(lane == b, exponent[b], exponents)
    exponents = exponents.astype(jnp.int32).astype(jnp.int16)
    for d in range(out_ref.shape[0]):
        out_ref[d, :blocks] = fixed
        out_ref[d, blocks] = exponents


def unpack(in_ref, out_ref, buf, sem):
    blocks = out_ref.shape[0]
    group = blocks // sem.shape[0]
    scales = []
    for t in range(in_ref.shape[0]):
        scales.append(jnp.exp2(in_ref[t, blocks].astype(jnp.int32).astype(F32) - BITS))
    copies = []
    for g in range(sem.shape[0]):
        for b in range(g * group, (g + 1) * group):
            for t, scale in enumerate(scales):
                buf[b, t] = in_ref[t, b].astype(jnp.int32).astype(F32) * scale[:, b : b + 1]
        part = pl.ds(g * group, group)
        copies.append(pltpu.make_async_copy(buf.at[part], out_ref.at[part], sem.at[g]))
        copies[-1].start()
    for copy in copies:
        copy.wait()


def body(tile_values, tile_coords, tile_owner, factor_b, factor_c):
    slots = tile_values.shape[0]
    edge = tile_values.shape[1]
    rank = factor_b.shape[1]
    shard = factor_b.shape[0]
    tiles_count = lax.axis_size("tiles")
    rows_count = lax.axis_size("rows")
    blocks = shard // edge
    tile = (STRIP, rank)

    chips = rows_count // CORES

    def from_peer(x, peer):
        return lax.ppermute(x, "rows", [(q, peer(q)) for q in range(rows_count)])

    def swap(x):
        groups = [[x * CORES + core for x in range(chips)] for core in range(CORES)]
        return lax.all_to_all(x, "rows", 0, 0, axis_index_groups=groups, tiled=True)

    sibling_b, sibling_c = (from_peer(f, lambda q: q ^ 1) for f in (factor_b, factor_c))
    by_block = lambda f: f.reshape(blocks, edge, rank)
    shards = jax.ShapeDtypeStruct((blocks, edge, rank), BF16)
    codes, rounds, shard_b, shard_c = pl.pallas_call(
        lambda *refs: plan(*refs, slots=slots, rows_count=rows_count, blocks=blocks),
        name="plan",
        out_shape=(
            jax.ShapeDtypeStruct((1, LANES), jnp.int32),
            jax.ShapeDtypeStruct((1, 1), jnp.int32),
            shards,
            shards,
        ),
        in_specs=[pl.BlockSpec(memory_space=pltpu.HBM)] * 4,
        out_specs=(vmem(), smem(), vmem(), vmem()),
        scratch_shapes=[
            pltpu.VMEM((1, tile_owner.shape[0]), jnp.int32),
            pltpu.VMEM((3, tile_owner.shape[0]), jnp.int32),
            pltpu.SemaphoreType.DMA((4,)),
        ],
        compiler_params=LIMIT,
    )(
        in_hbm(tile_owner.reshape(1, -1)),
        in_hbm(tile_coords.T),
        in_hbm(by_block(factor_b)),
        in_hbm(by_block(factor_c)),
    )
    sent = pl.pallas_call(
        lambda *refs: gather_factors(*refs, slots=slots),
        name="gather_factors",
        out_shape=tuple(jax.ShapeDtypeStruct((chips, c, edge, rank), BF16) for c in CAPACITIES),
        in_specs=[smem()] + [hbm()] * 4,
        out_specs=(pl.BlockSpec(memory_space=pltpu.HBM),) * len(CAPACITIES),
        scratch_shapes=[pltpu.SemaphoreType.DMA],
        compiler_params=LIMIT,
    )(
        codes,
        shard_b,
        shard_c,
        by_block(sibling_b),
        by_block(sibling_c),
    )
    rest = lax.cond(rounds[0, 0] > 0, swap, lambda x: x, sent[1])
    first, rest = lax.optimization_barrier((sent[0], rest))
    chosen = [swap(first), rest]
    own_x, own_b, own_c, sibling_b, sibling_c, *sent = lax.optimization_barrier(
        (tile_values, factor_b, factor_c, sibling_b, sibling_c, *sent)
    )
    gram = pl.pallas_call(
        chip_gram,
        name="chip_gram",
        out_shape=jax.ShapeDtypeStruct((rank, rank), F32),
        in_specs=[hbm()] * 4,
        out_specs=vmem(),
        scratch_shapes=[
            pltpu.VMEM((CORES, shard, rank), BF16),
            pltpu.SemaphoreType.DMA((CORES,)),
        ],
        compiler_params=LIMIT,
        cost_estimate=SMALL,
    )(in_hbm(own_b), in_hbm(own_c), sibling_b, sibling_c)
    gram = gram + from_peer(gram, lambda q: q ^ CORES)
    part = pl.pallas_call(
        load_part,
        name="load_part",
        out_shape=jax.ShapeDtypeStruct((edge // 2, edge, edge), BF16),
        in_specs=[pl.BlockSpec(memory_space=pltpu.HBM)],
        out_specs=vmem(),
        scratch_shapes=[pltpu.SemaphoreType.DMA],
        compiler_params=LIMIT,
        cost_estimate=SMALL,
    )(in_hbm(own_x))
    chosen, gram = lax.optimization_barrier((chosen, gram))

    partials = pl.pallas_call(
        lambda *refs: contract(*refs, slots=slots, blocks=blocks),
        name="contract",
        out_shape=jax.ShapeDtypeStruct((tiles_count, slots) + tile, F32),
        in_specs=[vmem(), pl.BlockSpec(memory_space=pltpu.HBM), vmem()] + [vmem()] * len(CAPACITIES),
        out_specs=pl.BlockSpec(memory_space=pltpu.HBM),
        scratch_shapes=[
            pltpu.VMEM((tiles_count, slots) + tile, F32),
            pltpu.VMEM(tile_values.shape, BF16),
            pltpu.VMEM((slots, edge, rank), F32),
            pltpu.VMEM((slots, edge, rank), BF16),
            pltpu.SMEM((1, LANES), jnp.int32),
            pltpu.SemaphoreType.DMA,
            pltpu.SemaphoreType.DMA((slots, PARTS)),
            pltpu.SemaphoreType.DMA((slots,)),
        ],
        compiler_params=pltpu.CompilerParams(vmem_limit_bytes=24 << 20),
        cost_estimate=pl.CostEstimate(flops=slots * 2 * edge**4, bytes_accessed=slots * 2 * edge**3, transcendentals=0),
    )(codes, in_hbm(tile_values), part, *chosen)
    moved = lax.all_to_all(partials, "tiles", 0, 0, tiled=True)
    gram = gram + from_peer(gram, lambda q: (chips - 1 - q // CORES) * CORES + q % CORES)
    moved, gram = lax.optimization_barrier((moved, gram))
    sums = jax.ShapeDtypeStruct((chips, blocks) + tile, F32)
    keep, send = pl.pallas_call(
        lambda *refs: gather_blocks(*refs, slots=slots),
        name="gather_blocks",
        out_shape=(sums, sums),
        in_specs=[smem(), vmem()],
        out_specs=(vmem(), vmem()),
        scratch_shapes=[pltpu.VMEM((CORES, chips, blocks) + tile, F32)],
        compiler_params=LIMIT,
    )(codes, moved)
    send, gram = lax.optimization_barrier((send, gram))
    other = from_peer(gram, lambda q: q ^ 1)
    summed, other = lax.optimization_barrier((keep + from_peer(send, lambda q: q ^ 1), other))
    owned = swap(summed)
    inverse = pl.pallas_call(
        invert,
        name="invert",
        out_shape=jax.ShapeDtypeStruct((rank, rank), F32),
        in_specs=[vmem()] * 2,
        out_specs=vmem(),
        compiler_params=LIMIT,
        cost_estimate=pl.CostEstimate(flops=1 << 30, bytes_accessed=1 << 20, transcendentals=64),
    )(gram, other)
    solved = pl.pallas_call(
        solve,
        name="solve",
        out_shape=jax.ShapeDtypeStruct((tiles_count, blocks + 1) + tile, jnp.int16),
        in_specs=[vmem(), vmem()],
        out_specs=vmem(),
        compiler_params=LIMIT,
    )(owned, inverse)
    full = lax.all_to_all(solved, "tiles", 0, 0, tiled=True)
    out = pl.pallas_call(
        unpack,
        name="unpack",
        out_shape=jax.ShapeDtypeStruct((blocks, tiles_count) + tile, F32),
        in_specs=[vmem()],
        out_specs=pl.BlockSpec(memory_space=pltpu.HBM),
        scratch_shapes=[
            pltpu.VMEM((blocks, tiles_count) + tile, F32),
            pltpu.SemaphoreType.DMA((4,)),
        ],
        compiler_params=LIMIT,
    )(full)
    return out.reshape(shard, rank)


def solution(mesh):
    in_specs = (P(("tiles", "rows"), None, None, None), P(), P(), P("rows", None), P("rows", None))
    out_specs = P("rows", None)
    return jax.shard_map(body, mesh=mesh, in_specs=in_specs, out_specs=out_specs, check_vma=False)
```
